128 devices in a mesh: angle: 16 (over y, x), block: 8 (over z, core).
Axes of the slice: x: 4, y: 4, z: 4, core: 2. Of those that a mesh axis runs over, the one named last changes fastest.
Arguments:
- object_field: float32 [32, 2, 512, 512], P(None, None, 'block'), may hold values from -1.5 to 1.5
- shears: int32 [16, 32], P('angle'), may hold values from -16 to 16, as said below
- positions: int32 [16, 8, 2], P('angle', 'block'), may hold values from 0 to 511
- measured: bfloat16 [16, 8, 512, 512], P('angle', 'block'), may hold values from 0 to 2
- probe_field: float32 [2, 512, 512], replicated
- kappa_field: float32 [16, 512, 512], P('angle'), may hold values from 0.01 to 0.1
Outputs:
- updated_object: float32 [32, 2, 512, 512], P(None, None, 'block')
The draws below stay inside these ranges and needn't reach their ends.
Inputs may be any that keep to these rules, and one draw needn't show every extreme that they name: `shears`: each angle's row offset of each slice; the values -16 and 16 occur in every draw.
All inputs are finite; a program needn't handle non-finite values.
Results may differ from the reference program's by a relative error of at most 0.0003.
Values sent between devices are 32-bit elements; how exact they have to be, the bound alone decides.
No kernel may reach another device: no remote copies, remote signals or barrier semaphores. Data moves between devices by JAX's collectives and lax.ppermute only.
A program may use at most 192 MiB of HBM per device.

```python
import math
import jax
import jax.numpy as jnp
from jax import lax

NX = 512
NY = 512
Z = 32
STEPS = 2
SH = 16
ANGLES = 16
FRAMES = 8


def draw_probe_field(key, part):
    coord_x = (jnp.arange(NX, dtype=jnp.float32) - NX / 2) / (NX / 4)
    coord_y = (jnp.arange(NY, dtype=jnp.float32) - NY / 2) / (NY / 4)
    envelope = 0.25 + jnp.exp(-0.5 * (coord_x[:, None] ** 2 + coord_y[None, :] ** 2))
    noise = jax.random.normal(key, (2, NX, NY), jnp.float32)
    return (1.2 * noise * envelope[None]).astype(jnp.float32)


def draw_shears(key, part):
    base_key, high_key, low_key = jax.random.split(key, 3)
    values = jax.random.randint(base_key, (ANGLES * Z,), -SH, SH + 1)
    high_index = jax.random.randint(high_key, (), 0, ANGLES * Z)
    low_index = (high_index + 1 + jax.random.randint(low_key, (), 0, ANGLES * Z - 1)) % (ANGLES * Z)
    values = values.at[high_index].set(SH).at[low_index].set(-SH)
    return values.reshape(ANGLES, Z).astype(jnp.int32)


def with_ends(drawn, stream_key, smallest, largest):
    spot = [jax.random.randint(jax.random.fold_in(stream_key, axis), (), 0, length) for axis, length in enumerate(drawn.shape)]
    longest = drawn.shape.index(max(drawn.shape))
    beside = spot[:longest] + [(spot[longest] + 1) % drawn.shape[longest]] + spot[longest + 1:]
    return drawn.at[tuple(spot)].set(smallest).at[tuple(beside)].set(largest)


def steps_of(stream_key, extent, cuts, low, largest):
    level, own = 1.0, jax.random.fold_in(stream_key, 6)
    for axis_at, blocks in cuts:
        draws = jnp.exp(jax.random.uniform(jax.random.fold_in(own, axis_at), (blocks,), jnp.float32, low / len(cuts), largest / len(cuts)))
        level = level * jnp.repeat(draws, extent[axis_at] // blocks).reshape([-1 if axis == axis_at else 1 for axis in range(len(extent))])
    return level


def scatter_about(own_key, extent, width, most, cuts=(), kind=jnp.bfloat16):
    gain = steps_of(own_key, extent, cuts, -0.22, 0.18) if cuts else 1.0
    values = jax.random.normal(own_key, extent, jnp.float32) * width * gain
    return jnp.minimum(jnp.maximum(values, -most), most).astype(kind)


def setup_inputs(seed: int = 0) -> dict:
    keys = jax.random.split(jax.random.key(seed), 7)
    return {
        "object_field": scatter_about(keys[0], (Z, 2, NX, NY), 0.25, 1.5, ((2, 8),), jnp.float32),
        "shears": draw_shears(jax.random.fold_in(keys[6], 71), 0),
        "positions": with_ends(jax.random.randint(keys[2], (ANGLES, FRAMES, 2), 0, NX), jax.random.fold_in(keys[2], 1), 0, NX - 1).astype(jnp.int32),
        "measured": jnp.clip(2.0 * jax.random.uniform(keys[3], (ANGLES, FRAMES, NX, NY), jnp.float32) ** steps_of(keys[3], (ANGLES, FRAMES, NX, NY), ((0, 16), (1, 8)), -0.2, 0.2), 0.0, 2.0).astype(jnp.bfloat16),
        "probe_field": draw_probe_field(jax.random.fold_in(keys[6], 71), 0),
        "kappa_field": jnp.clip(jnp.exp(math.log(0.1) - 2.3025851 * jax.random.uniform(keys[5], (ANGLES, NX, NY), jnp.float32) ** steps_of(keys[5], (ANGLES, NX, NY), ((0, 16),), -0.2, 0.2)), 0.01, 0.1),
    }


def laplace(field):
    return jnp.roll(field, 1, -2) + jnp.roll(field, -1, -2) + jnp.roll(field, 1, -1) + jnp.roll(field, -1, -1) - 4.0 * field

def frame_loss(projected, probe_field, kappa_row, offset, observed):
    window = jnp.roll(projected, (-offset[0], -offset[1]), axis=(1, 2))
    real_part = probe_field[0] * window[0] - probe_field[1] * window[1]
    imag_part = probe_field[0] * window[1] + probe_field[1] * window[0]
    for step in range(STEPS):
        real_part, imag_part = (real_part - kappa_row * laplace(imag_part), imag_part + kappa_row * laplace(real_part))
    misfit = real_part * real_part + imag_part * imag_part - observed.astype(jnp.float32)
    return 0.5 * jnp.sum(misfit * misfit)

def reference(object_field, shears, positions, measured, probe_field, kappa_field):
    intensity = probe_field[0] * probe_field[0] + probe_field[1] * probe_field[1]

    def per_angle(summed, inputs):
        shear_row, offsets, observed_all, kappa_row = inputs
        moved = jax.vmap(lambda slab, amount: jnp.roll(slab, -amount, axis=1))(object_field, shear_row)
        projected = lax.optimization_barrier(jnp.sum(moved, axis=0))

        def per_frame(totals, frame_in):
            offset, observed = frame_in
            grads = jax.grad(frame_loss)(projected, probe_field, kappa_row, offset, observed)
            weight = jnp.roll(intensity, (offset[0], offset[1]), axis=(0, 1))
            return (totals + jnp.concatenate([grads, weight[None]], 0), None)
        totals, _ = lax.scan(per_frame, jnp.zeros((3, NX, NY), jnp.float32), (offsets, observed_all))
        unsheared = jax.vmap(lambda amount: jnp.roll(totals, amount, axis=1))(shear_row)
        return (summed + unsheared, None)
    summed, _ = lax.scan(per_angle, jnp.zeros((Z, 3, NX, NY), jnp.float32), (shears, positions, measured, kappa_field))
    return object_field - summed[:, :2] / (summed[:, 2:3] + 1.0)
```

```python
import jax
import jax.numpy as jnp
from jax import lax
from jax.experimental import pallas as pl
from jax.experimental.pallas import tpu as pltpu
from jax.sharding import PartitionSpec as P

NX = 512
NY = 512
Z = 32
SH = 16
ANGLES = 16
FRAMES = 8
STRIP = 64
LANES = 128
COLS = NY // LANES
BASE = 24
ROWS = STRIP + 2 * BASE
RIM_ROWS = STRIP + 2 * SH
SENT = BASE + SH
WRAP = NX + ROWS
F32 = jnp.float32

SMEM = pl.BlockSpec(memory_space=pltpu.SMEM)
VMEM = pl.BlockSpec(memory_space=pltpu.VMEM)


def lane_block(c):
    return slice(c * LANES, (c + 1) * LANES)


def lane_ids(rows):
    return lax.broadcasted_iota(jnp.int32, (rows, LANES), 1)


def load_wrapped(scratch, index, image):
    for c in range(COLS):
        scratch[index + (c, pl.ds(0, NX))] = image[:, lane_block(c)]
        scratch[index + (c, pl.ds(NX, ROWS))] = image[:ROWS, lane_block(c)]


def rolled_blocks(scratch, index, first_row, rows, amount):
    whole, part = amount // LANES, amount % LANES
    turned = [
        pltpu.roll(scratch[index + ((c - whole) & (COLS - 1), pl.ds(first_row, rows))], part, 1)
        for c in range(COLS)
    ]
    keep = lane_ids(rows) >= part
    return [jnp.where(keep, turned[c], turned[c - 1]) for c in range(COLS)]


def measured_kernel(position, measured, out, wrapped):
    load_wrapped(wrapped, (), measured[...].astype(F32))
    for strip in range(FRAMES):
        first_row = (strip * STRIP - BASE - position[0]) & (NX - 1)
        for c, block in enumerate(rolled_blocks(wrapped, (), first_row, ROWS, position[1])):
            out[strip, c] = block


def project_kernel(shears, slices, out):
    step = pl.program_id(0)

    @pl.when(step == 0)
    def _():
        out[...] = jnp.zeros_like(out)

    count = slices.shape[0]
    for k in range(count):
        rows = pl.ds(SH - shears[step * count + k], STRIP)
        for part in range(2):
            for c in range(COLS):
                out[part, c, rows] += slices[k, part, :, lane_block(c)]


def frames_kernel(
    strip_index,
    positions,
    partial,
    before,
    after,
    measured,
    probe,
    kappa,
    out,
    wrapped,
    window,
    local,
    field_a,
    field_b,
    field_c,
):
    pad = 8
    load_wrapped(wrapped, (0,), probe[0])
    load_wrapped(wrapped, (1,), probe[1])
    load_wrapped(wrapped, (2,), kappa[...])
    window[:, :, pl.ds(BASE - SH, RIM_ROWS)] = partial[...]
    window[:, :, pl.ds(0, BASE - SH)] = jnp.zeros((2, COLS, BASE - SH, LANES), F32)
    window[:, :, pl.ds(ROWS - BASE + SH, BASE - SH)] = jnp.zeros((2, COLS, BASE - SH, LANES), F32)
    window[:, :, pl.ds(0, SENT)] += before[...]
    window[:, :, pl.ds(ROWS - SENT, SENT)] += after[...]
    out[...] = jnp.zeros_like(out)
    for field in (field_a, field_b, field_c):
        field[...] = jnp.zeros_like(field)
    tile = 16
    lanes = lane_ids(tile)
    first_lane = lanes == 0
    last_lane = lanes == LANES - 1

    def laplace(field, part, row):
        centre = [field[part, c, pl.ds(row, tile)] for c in range(COLS)]
        right = [pltpu.roll(v, 1, 1) for v in centre]
        left = [pltpu.roll(v, LANES - 1, 1) for v in centre]
        result = []
        for c in range(COLS):
            around = field[part, c, pl.ds(row - 1, tile)] + field[part, c, pl.ds(row + 1, tile)]
            around += jnp.where(first_lane, right[c - 1], right[c])
            around += jnp.where(last_lane, left[(c + 1) % COLS], left[c])
            result.append(around - 4.0 * centre[c])
        return centre, result

    def per_frame(frame, _):
        first_row = (strip_index[0] * STRIP - BASE - positions[frame, 0]) & (NX - 1)
        for k in range(3):
            for c, block in enumerate(
                rolled_blocks(wrapped, (k,), first_row, ROWS, positions[frame, 1])
            ):
                local[k, c] = block

        def over_rows(body):
            def one(i, _):
                row = pl.multiple_of(i * tile, tile)
                body(row, pl.multiple_of(row + pad, pad))
                return 0

            lax.fori_loop(0, ROWS // tile, one, 0)

        def leave(row, padded):
            for c in range(COLS):
                probe_re, probe_im = (local[k, c, pl.ds(row, tile)] for k in range(2))
                re, im = (window[k, c, pl.ds(row, tile)] for k in range(2))
                field_a[0, c, pl.ds(padded, tile)] = probe_re * re - probe_im * im
                field_a[1, c, pl.ds(padded, tile)] = probe_re * im + probe_im * re

        def forward(row, padded):
            re, lap_re = laplace(field_a, 0, padded)
            im, lap_im = laplace(field_a, 1, padded)
            for c in range(COLS):
                kappa_row = local[2, c, pl.ds(row, tile)]
                field_b[0, c, pl.ds(padded, tile)] = re[c] - kappa_row * lap_im[c]
                field_b[1, c, pl.ds(padded, tile)] = im[c] + kappa_row * lap_re[c]

        def turn(row, padded):
            re, lap_re = laplace(field_b, 0, padded)
            im, lap_im = laplace(field_b, 1, padded)
            for c in range(COLS):
                kappa_row = local[2, c, pl.ds(row, tile)]
                wave_re = re[c] - kappa_row * lap_im[c]
                wave_im = im[c] + kappa_row * lap_re[c]
                observed = measured[frame, c, pl.ds(row, tile)]
                twice = 2.0 * (wave_re * wave_re + wave_im * wave_im - observed)
                grad_re, grad_im = twice * wave_re, twice * wave_im
                field_a[0, c, pl.ds(padded, tile)] = grad_re
                field_a[1, c, pl.ds(padded, tile)] = grad_im
                field_c[0, c, pl.ds(padded, tile)] = kappa_row * grad_re
                field_c[1, c, pl.ds(padded, tile)] = kappa_row * grad_im

        def backward(row, padded):
            _, lap_re = laplace(field_c, 0, padded)
            _, lap_im = laplace(field_c, 1, padded)
            for c in range(COLS):
                kappa_row = local[2, c, pl.ds(row, tile)]
                grad_re = field_a[0, c, pl.ds(padded, tile)] + lap_im[c]
                grad_im = field_a[1, c, pl.ds(padded, tile)] - lap_re[c]
                field_a[0, c, pl.ds(padded, tile)] = grad_re
                field_a[1, c, pl.ds(padded, tile)] = grad_im
                field_b[0, c, pl.ds(padded, tile)] = kappa_row * grad_re
                field_b[1, c, pl.ds(padded, tile)] = kappa_row * grad_im

        def collect(i, _):
            row = pl.multiple_of(i * tile, tile)
            inner = pl.multiple_of(row + BASE - SH, pad)
            padded = pl.multiple_of(inner + pad, pad)
            _, lap_re = laplace(field_b, 0, padded)
            _, lap_im = laplace(field_b, 1, padded)
            for c in range(COLS):
                grad_re = field_a[0, c, pl.ds(padded, tile)] + lap_im[c]
                grad_im = field_a[1, c, pl.ds(padded, tile)] - lap_re[c]
                probe_re, probe_im = (local[k, c, pl.ds(inner, tile)] for k in range(2))
                out[0, c, pl.ds(row, tile)] += probe_re * grad_re + probe_im * grad_im
                out[1, c, pl.ds(row, tile)] += probe_re * grad_im - probe_im * grad_re
            return 0

        over_rows(leave)
        over_rows(forward)
        over_rows(turn)
        over_rows(backward)
        lax.fori_loop(0, RIM_ROWS // tile, collect, 0)
        return 0

    lax.fori_loop(0, FRAMES, per_frame, 0)


def weight_kernel(strip_index, positions, probe, out, wrapped):
    load_wrapped(wrapped, (), probe[0] * probe[0] + probe[1] * probe[1])

    def per_angle(angle, _):
        total = [jnp.zeros((RIM_ROWS, LANES), F32)] * COLS
        for frame in range(FRAMES):
            first_row = (strip_index[0] * STRIP - SH - positions[angle, frame, 0]) & (NX - 1)
            blocks = rolled_blocks(wrapped, (), first_row, RIM_ROWS, positions[angle, frame, 1])
            total = [a + b for a, b in zip(total, blocks)]
        for c in range(COLS):
            out[angle, c] = total[c]
        return 0

    lax.fori_loop(0, ANGLES, per_angle, 0)


def divisor_kernel(shears, weights, out):
    base = pl.program_id(0) * out.shape[0]

    def per_slice(k, _):
        starts = [SH - shears[a, base + k] for a in range(ANGLES)]
        for c in range(COLS):
            total = jnp.ones((STRIP, LANES), F32)
            for a in range(ANGLES):
                total += weights[a, c, pl.ds(starts[a], STRIP)]
            out[k, :, lane_block(c)] = 1.0 / total
        return 0

    lax.fori_loop(0, out.shape[0], per_slice, 0)


def update_kernel(shears, grads, slices, scale, out):
    base = pl.program_id(0) * out.shape[0]

    def per_slice(k, _):
        starts = [SH - shears[a, base + k] for a in range(ANGLES)]
        for part in range(2):
            for c in range(COLS):
                total = grads[0, part, c, pl.ds(starts[0], STRIP)]
                for a in range(1, ANGLES):
                    total += grads[a, part, c, pl.ds(starts[a], STRIP)]
                cols = lane_block(c)
                out[k, part, :, cols] = slices[k, part, :, cols] - total * scale[k, :, cols]
        return 0

    lax.fori_loop(0, out.shape[0], per_slice, 0)


def per_device(object_field, shears, positions, measured, probe_field, kappa_field):
    strip_index = lax.axis_index("block").astype(jnp.int32)[None]
    all_shears = lax.all_gather(shears[0], "angle", axis=0)
    all_positions = lax.all_gather(positions[0, 0], ("angle", "block"), axis=0)
    all_positions = all_positions.reshape(ANGLES, FRAMES, 2)
    own_positions = lax.dynamic_index_in_dim(
        all_positions, lax.axis_index("angle"), 0, keepdims=False
    )

    moved = pl.pallas_call(
        measured_kernel,
        out_shape=jax.ShapeDtypeStruct((FRAMES, COLS, ROWS, LANES), F32),
        in_specs=[SMEM, VMEM],
        out_specs=VMEM,
        scratch_shapes=[pltpu.VMEM((COLS, WRAP, LANES), F32)],
        name="measured_rows",
    )(positions[0, 0], measured[0, 0])
    observed = lax.all_to_all(moved, "block", 0, 0)

    step = 4
    partial = pl.pallas_call(
        project_kernel,
        grid=(Z // step,),
        out_shape=jax.ShapeDtypeStruct((2, COLS, RIM_ROWS, LANES), F32),
        in_specs=[SMEM, pl.BlockSpec((step, 2, STRIP, NY), lambda i: (i, 0, 0, 0))],
        out_specs=pl.BlockSpec((2, COLS, RIM_ROWS, LANES), lambda i: (0, 0, 0, 0)),
        name="project",
    )(shears[0], object_field)
    count = FRAMES
    up = [(i, (i + 1) % count) for i in range(count)]
    down = [(j, i) for i, j in up]
    before = lax.ppermute(partial[:, :, RIM_ROWS - SENT :], "block", up)
    after = lax.ppermute(partial[:, :, :SENT], "block", down)

    field = pltpu.VMEM((2, COLS, ROWS + 16, LANES), F32)
    grads = pl.pallas_call(
        frames_kernel,
        out_shape=jax.ShapeDtypeStruct((2, COLS, RIM_ROWS, LANES), F32),
        in_specs=[SMEM, SMEM] + [VMEM] * 6,
        out_specs=VMEM,
        scratch_shapes=[
            pltpu.VMEM((3, COLS, WRAP, LANES), F32),
            pltpu.VMEM((2, COLS, ROWS, LANES), F32),
            pltpu.VMEM((3, COLS, ROWS, LANES), F32),
            field,
            field,
            field,
        ],
        name="frames",
    )(
        strip_index,
        own_positions,
        partial,
        before,
        after,
        observed,
        probe_field,
        kappa_field[0],
    )

    weights = pl.pallas_call(
        weight_kernel,
        out_shape=jax.ShapeDtypeStruct((ANGLES, COLS, RIM_ROWS, LANES), F32),
        in_specs=[SMEM, SMEM, VMEM],
        out_specs=VMEM,
        scratch_shapes=[pltpu.VMEM((COLS, WRAP, LANES), F32)],
        name="weights",
    )(strip_index, all_positions, probe_field)
    slices_spec = pl.BlockSpec((step, STRIP, NY), lambda i: (i, 0, 0))
    scale = pl.pallas_call(
        divisor_kernel,
        grid=(Z // step,),
        out_shape=jax.ShapeDtypeStruct((Z, STRIP, NY), F32),
        in_specs=[SMEM, VMEM],
        out_specs=slices_spec,
        name="divisor",
    )(all_shears, weights)

    all_grads = lax.all_gather(grads, "angle", axis=0)
    object_spec = pl.BlockSpec((step, 2, STRIP, NY), lambda i: (i, 0, 0, 0))
    return pl.pallas_call(
        update_kernel,
        grid=(Z // step,),
        out_shape=jax.ShapeDtypeStruct(object_field.shape, F32),
        in_specs=[SMEM, VMEM, object_spec, slices_spec],
        out_specs=object_spec,
        name="update",
    )(all_shears, all_grads, object_field, scale)


def solution(mesh):
    placed = (
        P(None, None, "block", None),
        P("angle", None),
        P("angle", "block", None),
        P("angle", "block", None, None),
        P(),
        P("angle", None, None),
    )
    return jax.shard_map(
        per_device,
        mesh=mesh,
        in_specs=placed,
        out_specs=P(None, None, "block", None),
        check_vma=False,
    )
```

```python
import jax
import jax.numpy as jnp
from jax import lax
from jax.experimental import pallas as pl
from jax.experimental.pallas import tpu as pltpu
from jax.sharding import PartitionSpec as P

NX = 512
NY = 512
Z = 32
SH = 16
ANGLES = 16
FRAMES = 8
STRIP = 64
LANES = 128
COLS = NY // LANES
BASE = 8
ROWS = STRIP + 2 * BASE
RIM_ROWS = STRIP + 2 * SH
SENT = BASE + SH
WRAP = NX + RIM_ROWS
F32 = jnp.float32
BF16 = jnp.bfloat16
HOPS = (0, 2, 1, 3)
SIDE = 4
COST_SCALE = 3_000_000

SMEM = pl.BlockSpec(memory_space=pltpu.SMEM)
VMEM = pl.BlockSpec(memory_space=pltpu.VMEM)


def cost(microseconds):
    return pl.CostEstimate(
        flops=0, transcendentals=0, bytes_accessed=microseconds * COST_SCALE
    )


def lane_block(c):
    return slice(c * LANES, (c + 1) * LANES)


def lane_ids(rows):
    return lax.broadcasted_iota(jnp.int32, (rows, LANES), 1)


def load_wrapped(scratch, index, image):
    for c in range(COLS):
        scratch[index + (c, pl.ds(0, NX))] = image[:, lane_block(c)]
        scratch[index + (c, pl.ds(NX, WRAP - NX))] = image[: WRAP - NX, lane_block(c)]


def rolled_blocks(scratch, index, first_row, rows, amount):
    whole, part = amount // LANES, amount % LANES
    turned = [
        pltpu.roll(scratch[index + ((c - whole) & (COLS - 1), pl.ds(first_row, rows))], part, 1)
        for c in range(COLS)
    ]
    keep = lane_ids(rows) >= part
    return [jnp.where(keep, turned[c], turned[c - 1]) for c in range(COLS)]


def interleave(transposed=False):
    old = lax.broadcasted_iota(jnp.int32, (NY, NY), 1 if transposed else 0)
    new = lax.broadcasted_iota(jnp.int32, (NY, NY), 0 if transposed else 1)
    return jnp.where(old == (new % LANES) * COLS + new // LANES, 1.0, 0.0).astype(BF16)


def permuted(image, matrix):
    result = None
    for term in range(3):
        high = image.astype(BF16)
        product = jnp.dot(high, matrix, preferred_element_type=F32)
        result = product if result is None else result + product
        if term < 2:
            image = image - high.astype(F32)
    return result


def interleaved_roll(scratch, index, first_row, rows, amount):
    whole, part = amount // COLS, amount % COLS
    return [
        pltpu.roll(
            scratch[index + ((c - part) & (COLS - 1), pl.ds(first_row, rows))],
            (whole + jnp.where(c < part, 1, 0)) & (LANES - 1),
            1,
        )
        for c in range(COLS)
    ]


def measured_kernel(position, measured, out, wrapped):
    load_wrapped(
        wrapped, (), jnp.dot(measured[...], interleave(), preferred_element_type=F32)
    )
    for strip in range(FRAMES):
        first_row = (strip * STRIP - BASE - position[0]) & (NX - 1)
        for c, block in enumerate(interleaved_roll(wrapped, (), first_row, ROWS, position[1])):
            out[strip, c] = block
        for k in range(2):
            out[strip, 0, k : k + 1] = jnp.full((1, LANES), position[k].astype(F32), F32)


def project_kernel(shears, slices, out):
    step = pl.program_id(0)

    @pl.when(step == 0)
    def _():
        out[...] = jnp.zeros_like(out)

    count = slices.shape[0]
    for k in range(count):
        rows = pl.ds(SH - shears[step * count + k], STRIP)
        for part in range(2):
            for c in range(COLS):
                out[part, c, rows] += slices[k, part, :, lane_block(c)]

    @pl.when(step == pl.num_programs(0) - 1)
    def _():
        matrix = interleave()
        for part in range(2):
            image = jnp.concatenate([out[part, c] for c in range(COLS)], axis=1)
            image = permuted(image, matrix)
            for c in range(COLS):
                out[part, c] = image[:, lane_block(c)]


def fields_kernel(probe, kappa, out):
    matrix = interleave()
    for k in range(3):
        load_wrapped(out, (k,), permuted(probe[k] if k < 2 else kappa[...], matrix))


def frames_kernel(
    strip_index,
    partial,
    before,
    after,
    measured,
    wrapped,
    out,
    window,
    local,
    field_a,
    field_b,
    field_c,
    total,
    positions,
):
    pad = 8
    for frame in range(FRAMES):
        for k in range(2):
            place = jnp.max(measured[frame, 0, k : k + 1])
            positions[frame, k] = place.astype(jnp.int32)
    window[...] = partial[:, :, SH - BASE : SH - BASE + ROWS]
    window[:, :, :SENT] += before[...]
    window[:, :, ROWS - SENT :] += after[...]
    total[...] = jnp.zeros_like(total)
    for field in (field_a, field_b, field_c):
        field[:, :, :pad] = jnp.zeros((2, COLS, pad, LANES), F32)
        field[:, :, pad + ROWS :] = jnp.zeros((2, COLS, pad, LANES), F32)
    tile = 16

    def laplace(field, part, row):
        centre = field[part, :, pl.ds(row, tile)]
        around = field[part, :, pl.ds(row - 1, tile)] + field[part, :, pl.ds(row + 1, tile)]
        left = jnp.concatenate([pltpu.roll(centre[COLS - 1 :], 1, 2), centre[: COLS - 1]], axis=0)
        right = jnp.concatenate([centre[1:], pltpu.roll(centre[:1], LANES - 1, 2)], axis=0)
        return centre, around + left + right - 4.0 * centre

    def per_frame(frame, _):
        first_row = (strip_index[0] * STRIP - BASE - positions[frame, 0]) & (NX - 1)
        for k in range(3):
            for c, block in enumerate(
                interleaved_roll(wrapped, (k,), first_row, ROWS, positions[frame, 1])
            ):
                local[k, c] = block
        tiles = range(0, ROWS, tile)
        for row in tiles:
            rows, padded = pl.ds(row, tile), pl.ds(row + pad, tile)
            probe_re, probe_im = local[0, :, rows], local[1, :, rows]
            re, im = window[0, :, rows], window[1, :, rows]
            field_a[0, :, padded] = probe_re * re - probe_im * im
            field_a[1, :, padded] = probe_re * im + probe_im * re
        for row in tiles:
            rows, padded = pl.ds(row, tile), pl.ds(row + pad, tile)
            re, lap_re = laplace(field_a, 0, row + pad)
            im, lap_im = laplace(field_a, 1, row + pad)
            kappa = local[2, :, rows]
            field_b[0, :, padded] = re - kappa * lap_im
            field_b[1, :, padded] = im + kappa * lap_re
        for row in tiles:
            rows, padded = pl.ds(row, tile), pl.ds(row + pad, tile)
            re, lap_re = laplace(field_b, 0, row + pad)
            im, lap_im = laplace(field_b, 1, row + pad)
            kappa = local[2, :, rows]
            wave_re = re - kappa * lap_im
            wave_im = im + kappa * lap_re
            twice = 2.0 * (wave_re * wave_re + wave_im * wave_im - measured[frame, :, rows])
            grad_re, grad_im = twice * wave_re, twice * wave_im
            field_a[0, :, padded] = grad_re
            field_a[1, :, padded] = grad_im
            field_c[0, :, padded] = kappa * grad_re
            field_c[1, :, padded] = kappa * grad_im
        for row in tiles:
            rows, padded = pl.ds(row, tile), pl.ds(row + pad, tile)
            _, lap_re = laplace(field_c, 0, row + pad)
            _, lap_im = laplace(field_c, 1, row + pad)
            kappa = local[2, :, rows]
            grad_re = field_a[0, :, padded] + lap_im
            grad_im = field_a[1, :, padded] - lap_re
            field_a[0, :, padded] = grad_re
            field_a[1, :, padded] = grad_im
            field_b[0, :, padded] = kappa * grad_re
            field_b[1, :, padded] = kappa * grad_im
        for row in range(0, STRIP, tile):
            rows, padded = pl.ds(row + BASE, tile), pl.ds(row + BASE + pad, tile)
            _, lap_re = laplace(field_b, 0, row + BASE + pad)
            _, lap_im = laplace(field_b, 1, row + BASE + pad)
            grad_re = field_a[0, :, padded] + lap_im
            grad_im = field_a[1, :, padded] - lap_re
            probe_re, probe_im = local[0, :, rows], local[1, :, rows]
            total[0, :, pl.ds(row, tile)] += probe_re * grad_re + probe_im * grad_im
            total[1, :, pl.ds(row, tile)] += probe_re * grad_im - probe_im * grad_re
        return 0

    lax.fori_loop(0, FRAMES, per_frame, 0)
    matrix = interleave(transposed=True)
    for part in range(2):
        image = jnp.concatenate([total[part, c] for c in range(COLS)], axis=1)
        image = permuted(image, matrix)
        for c in range(COLS):
            out[part, c] = image[:, lane_block(c)]


def weight_kernel(strip_index, positions, probe, out, wrapped):
    load_wrapped(wrapped, (), probe[0] * probe[0] + probe[1] * probe[1])
    chunk = 32

    def per_angle(angle, _):
        for row in range(0, RIM_ROWS, chunk):
            total = [jnp.zeros((chunk, LANES), F32)] * COLS
            for frame in range(FRAMES):
                first_row = (strip_index[0] * STRIP - SH - positions[angle, frame, 0]) & (NX - 1)
                blocks = rolled_blocks(
                    wrapped, (), first_row + row, chunk, positions[angle, frame, 1]
                )
                total = [a + b for a, b in zip(total, blocks)]
            for c in range(COLS):
                out[angle, c, row : row + chunk] = total[c]
        return 0

    lax.fori_loop(0, ANGLES, per_angle, 0)


def divisor_kernel(shears, weights, out):
    base = pl.program_id(0) * out.shape[0]

    def per_slice(k, _):
        starts = [SH - shears[a, base + k] for a in range(ANGLES)]
        for c in range(COLS):
            total = jnp.ones((STRIP, LANES), F32)
            for a in range(ANGLES):
                total += weights[a, c, pl.ds(starts[a], STRIP)]
            out[k, :, lane_block(c)] = 1.0 / total
        return 0

    lax.fori_loop(0, out.shape[0], per_slice, 0)


def split(values):
    high = values.astype(BF16)
    return high, (values - high.astype(F32)).astype(BF16)


def core_kernel(shears, own, two, one, three, slices, scale, out, grads):
    @pl.when(pl.program_id(0) == 0)
    def _():
        for k, piece in enumerate((own, two, one, three)):
            for j in range(SIDE):
                grads[SIDE * k + j, :, :, SH : SH + STRIP] = piece[j]
        grads[:, :, :, :SH] = jnp.zeros((ANGLES, 2, COLS, SH, LANES), F32)
        grads[:, :, :, SH + STRIP :] = jnp.zeros((ANGLES, 2, COLS, SH, LANES), F32)

    base = pl.program_id(0) * out.shape[0]

    def per_slice(k, _):
        starts = [SH - shears[a, base + k] for a in range(ANGLES)]
        for part in range(2):
            for c in range(COLS):
                total = grads[0, part, c, pl.ds(starts[0], STRIP)]
                for a in range(1, ANGLES):
                    total += grads[a, part, c, pl.ds(starts[a], STRIP)]
                cols = lane_block(c)
                out[k, part, :, cols] = slices[k, part, :, cols] - total * scale[k, :, cols]
        return 0

    lax.fori_loop(0, out.shape[0], per_slice, 0)


def rim_kernel(shears, before, after, scale, core, out, high, low, shifts):
    side = pl.program_id(0)

    def take(rim):
        for a in range(ANGLES):
            for part in range(2):
                for c in range(COLS):
                    rows, cols = slice(a * SH, (a + 1) * SH), lane_block(part * COLS + c)
                    high[rows, cols], low[rows, cols] = split(rim[a, part, c])

    @pl.when((pl.program_id(1) == 0) & (side == 0))
    def _():
        take(before)

    @pl.when((pl.program_id(1) == 0) & (side == 1))
    def _():
        take(after)

    count = out.shape[0]
    width = ANGLES * SH
    column = lax.broadcasted_iota(jnp.int32, (SH, width), 1) & (SH - 1)
    apart = column - lax.broadcasted_iota(jnp.int32, (SH, width), 0)
    middle = jnp.where(side == 0, SH, -SH)
    for k in range(count):
        chosen = jnp.where(apart == middle - shears[k : k + 1], 1.0, 0.0)
        shifts[k * SH : (k + 1) * SH] = chosen.astype(BF16)
    product = jnp.dot(shifts[...], high[...], preferred_element_type=F32)
    product += jnp.dot(shifts[...], low[...], preferred_element_type=F32)
    for k in range(count):
        for part in range(2):
            total = product[k * SH : (k + 1) * SH, part * NY : (part + 1) * NY]
            out[k, part] = core[k, part] - total * scale[k]


def hop_pairs(hop, stage):
    pairs = []
    for y in range(SIDE):
        for x in range(SIDE):
            for block in range(FRAMES):
                along_x = (block % 2 == 0) == (stage == 0)
                to_y = y if along_x else (y + hop) % SIDE
                to_x = (x + hop) % SIDE if along_x else x
                pairs.append(((y * SIDE + x) * FRAMES + block, (to_y * SIDE + to_x) * FRAMES + block))
    return pairs


def gather_angles(grads, facts):
    axes = ("angle", "block")
    row = [grads] + [lax.ppermute(grads, axes, hop_pairs(hop, 0)) for hop in HOPS[1:]]
    row, facts = lax.optimization_barrier((jnp.stack(row), facts))
    pieces = [row] + [lax.ppermute(row, axes, hop_pairs(hop, 1)) for hop in HOPS[1:]]
    angle = lax.axis_index("angle")
    y, x = angle // SIDE, angle % SIDE
    odd = lax.axis_index("block") % 2
    second, first = (jnp.asarray(HOPS).repeat(SIDE), jnp.asarray(HOPS * SIDE))
    along_x = jnp.where(odd == 1, second, first)
    along_y = jnp.where(odd == 1, first, second)
    order = ((y - along_y) % SIDE) * SIDE + (x - along_x) % SIDE
    return pieces, order.astype(jnp.int32), facts


def per_device(object_field, shears, positions, measured, probe_field, kappa_field):
    strip_index = lax.axis_index("block").astype(jnp.int32)[None]
    moved = pl.pallas_call(
        measured_kernel,
        out_shape=jax.ShapeDtypeStruct((FRAMES, COLS, ROWS, LANES), F32),
        in_specs=[SMEM, VMEM],
        out_specs=VMEM,
        scratch_shapes=[pltpu.VMEM((COLS, WRAP, LANES), F32)],
        cost_estimate=cost(3),
        name="measured_rows",
    )(positions[0, 0], measured[0, 0])
    observed = lax.all_to_all(moved, "block", 0, 0)
    facts = observed[:, 0, :2, 0].reshape(2 * FRAMES).astype(jnp.int32)
    facts = jnp.pad(jnp.concatenate([facts, shears[0]]), (0, LANES - 2 * FRAMES - Z))
    facts = jnp.broadcast_to(facts, (ANGLES, 8, LANES))
    facts, observed = lax.optimization_barrier((facts, observed))

    step = 4
    partial = pl.pallas_call(
        project_kernel,
        grid=(Z // step,),
        out_shape=jax.ShapeDtypeStruct((2, COLS, RIM_ROWS, LANES), F32),
        in_specs=[SMEM, pl.BlockSpec((step, 2, STRIP, NY), lambda i: (i, 0, 0, 0))],
        out_specs=pl.BlockSpec((2, COLS, RIM_ROWS, LANES), lambda i: (0, 0, 0, 0)),
        cost_estimate=cost(7),
        name="project",
    )(shears[0], object_field)
    count = FRAMES
    up = [(i, (i + 1) % count) for i in range(count)]
    down = [(j, i) for i, j in up]
    before = lax.ppermute(partial[:, :, RIM_ROWS - SENT :], "block", up)
    after = lax.ppermute(partial[:, :, :SENT], "block", down)
    wrapped = pl.pallas_call(
        fields_kernel,
        out_shape=jax.ShapeDtypeStruct((3, COLS, WRAP, LANES), F32),
        in_specs=[VMEM, VMEM],
        out_specs=VMEM,
        cost_estimate=cost(6),
        name="fields",
    )(probe_field, kappa_field[0])

    field = pltpu.VMEM((2, COLS, ROWS + 16, LANES), F32)
    grads = pl.pallas_call(
        frames_kernel,
        out_shape=jax.ShapeDtypeStruct((2, COLS, STRIP, LANES), F32),
        in_specs=[SMEM] + [VMEM] * 5,
        out_specs=VMEM,
        scratch_shapes=[
            pltpu.VMEM((2, COLS, ROWS, LANES), F32),
            pltpu.VMEM((3, COLS, ROWS, LANES), F32),
            field,
            field,
            field,
            pltpu.VMEM((2, COLS, STRIP, LANES), F32),
            pltpu.SMEM((FRAMES, 2), jnp.int32),
        ],
        cost_estimate=cost(9),
        name="frames",
    )(strip_index, partial, before, after, observed, wrapped)
    facts, grads = lax.optimization_barrier((facts, grads))
    facts = lax.all_to_all(facts, "angle", 0, 0)
    pieces, order, facts = gather_angles(grads, facts)
    facts = facts[:, 0]
    all_positions = facts[:, : 2 * FRAMES].reshape(ANGLES, FRAMES, 2)
    all_shears = facts[:, 2 * FRAMES : 2 * FRAMES + Z]
    ordered_shears = jnp.take(all_shears, order, axis=0)
    rim_shears = ordered_shears.reshape(SIDE, SIDE, Z).transpose(2, 1, 0).reshape(Z, ANGLES)
    rim_shears = jnp.repeat(rim_shears, SH, axis=1)
    weights = pl.pallas_call(
        weight_kernel,
        out_shape=jax.ShapeDtypeStruct((ANGLES, COLS, RIM_ROWS, LANES), F32),
        in_specs=[SMEM, SMEM, VMEM],
        out_specs=VMEM,
        scratch_shapes=[pltpu.VMEM((COLS, WRAP, LANES), F32)],
        cost_estimate=cost(2),
        name="weights",
    )(strip_index, all_positions, probe_field)
    slices_spec = pl.BlockSpec((step, STRIP, NY), lambda i: (i, 0, 0))
    scale = pl.pallas_call(
        divisor_kernel,
        grid=(Z // step,),
        out_shape=jax.ShapeDtypeStruct((Z, STRIP, NY), F32),
        in_specs=[SMEM, VMEM],
        out_specs=slices_spec,
        cost_estimate=cost(2),
        name="divisor",
    )(all_shears, weights)

    scale, *pieces = lax.optimization_barrier((scale, *pieces))
    rims = [
        jnp.concatenate([piece[..., rows, :] for piece in pieces])
        for rows in (slice(STRIP - SH, STRIP), slice(0, SH))
    ]
    rims = [lax.ppermute(rim, "block", pairs) for rim, pairs in zip(rims, (up, down))]

    object_spec = pl.BlockSpec((step, 2, STRIP, NY), lambda i: (i, 0, 0, 0))
    core = pl.pallas_call(
        core_kernel,
        grid=(Z // step,),
        out_shape=jax.ShapeDtypeStruct(object_field.shape, F32),
        in_specs=[SMEM] + [VMEM] * 4 + [object_spec, slices_spec],
        out_specs=object_spec,
        scratch_shapes=[pltpu.VMEM((ANGLES, 2, COLS, RIM_ROWS, LANES), F32)],
        cost_estimate=cost(17),
        name="core",
    )(ordered_shears, *pieces, object_field, scale)
    many = 16
    edge_spec = pl.BlockSpec((many, 2, SH, NY), lambda j, i: (i, 0, j * (STRIP // SH - 1), 0))
    return pl.pallas_call(
        rim_kernel,
        grid=(2, Z // many),
        out_shape=jax.ShapeDtypeStruct(object_field.shape, F32),
        in_specs=[pl.BlockSpec((many, ANGLES * SH), lambda j, i: (i, 0)), VMEM, VMEM]
        + [pl.BlockSpec((many, SH, NY), lambda j, i: (i, j * (STRIP // SH - 1), 0)), edge_spec],
        out_specs=edge_spec,
        scratch_shapes=[
            pltpu.VMEM((ANGLES * SH, 2 * NY), BF16),
            pltpu.VMEM((ANGLES * SH, 2 * NY), BF16),
            pltpu.VMEM((many * SH, ANGLES * SH), BF16),
        ],
        input_output_aliases={4: 0},
        cost_estimate=cost(9),
        name="rim",
    )(rim_shears, *rims, scale, core)


def solution(mesh):
    placed = (
        P(None, None, "block", None),
        P("angle", None),
        P("angle", "block", None),
        P("angle", "block", None, None),
        P(),
        P("angle", None, None),
    )
    return jax.shard_map(
        per_device,
        mesh=mesh,
        in_specs=placed,
        out_specs=P(None, None, "block", None),
        check_vma=False,
    )
```

```python
import jax
import jax.numpy as jnp
from jax import lax
from jax.experimental import pallas as pl
from jax.experimental.pallas import tpu as pltpu
from jax.sharding import PartitionSpec as P

NX = 512
NY = 512
Z = 32
SH = 16
ANGLES = 16
FRAMES = 8
STRIP = 64
LANES = 128
COLS = NY // LANES
BASE = 8
ROWS = STRIP + 2 * BASE
RIM_ROWS = STRIP + 2 * SH
SENT = BASE + SH
WRAP = NX + RIM_ROWS
F32 = jnp.float32
BF16 = jnp.bfloat16
HOPS = (2, 1, 3)
SIDE = 4
BLOCKS = 2 * COLS
COST_SCALE = 3_000_000

SMEM = pl.BlockSpec(memory_space=pltpu.SMEM)
VMEM = pl.BlockSpec(memory_space=pltpu.VMEM)


def cost(microseconds):
    return pl.CostEstimate(
        flops=0, transcendentals=0, bytes_accessed=microseconds * COST_SCALE
    )


def vmem(mebibytes):
    return pltpu.CompilerParams(vmem_limit_bytes=mebibytes * 2**20)


def lane_block(c):
    return slice(c * LANES, (c + 1) * LANES)


def lane_ids(rows):
    return lax.broadcasted_iota(jnp.int32, (rows, LANES), 1)


def load_wrapped(scratch, index, image):
    for c in range(COLS):
        scratch[index + (c, pl.ds(0, NX))] = image[:, lane_block(c)]
        scratch[index + (c, pl.ds(NX, WRAP - NX))] = image[: WRAP - NX, lane_block(c)]


def interleave(transposed=False):
    old = lax.broadcasted_iota(jnp.int32, (NY, NY), 1 if transposed else 0)
    new = lax.broadcasted_iota(jnp.int32, (NY, NY), 0 if transposed else 1)
    return jnp.where(old == (new % LANES) * COLS + new // LANES, 1.0, 0.0).astype(BF16)


def permuted(image, matrix):
    result = None
    for term in range(3):
        high = image.astype(BF16)
        product = jnp.dot(high, matrix, preferred_element_type=F32)
        result = product if result is None else result + product
        if term < 2:
            image = image - high.astype(F32)
    return result


def interleaved_roll(scratch, index, first_row, rows, amount):
    whole, part = amount >> 2, amount & (COLS - 1)
    return [
        pltpu.roll(
            scratch[index + ((c - part) & (COLS - 1), pl.ds(first_row, rows))],
            (whole + jnp.where(c < part, 1, 0)) & (LANES - 1),
            1,
        )
        for c in range(COLS)
    ]


def measured_kernel(position, measured, out, wrapped):
    load_wrapped(
        wrapped, (), jnp.dot(measured[...], interleave(), preferred_element_type=F32)
    )
    for strip in range(FRAMES):
        first_row = (strip * STRIP - BASE - position[0]) & (NX - 1)
        for c, block in enumerate(interleaved_roll(wrapped, (), first_row, ROWS, position[1])):
            out[strip, c] = block
        for k in range(2):
            out[strip, 0, k : k + 1] = jnp.full((1, LANES), position[k].astype(F32), F32)


def project_kernel(shears, slices, out):
    step = pl.program_id(0)

    @pl.when(step == 0)
    def _():
        out[...] = jnp.zeros_like(out)

    count = slices.shape[0]
    for k in range(count):
        rows = pl.ds(SH - shears[step * count + k], STRIP)
        for part in range(2):
            for c in range(COLS):
                out[part, c, rows] += slices[k, part, :, lane_block(c)]

    @pl.when(step == pl.num_programs(0) - 1)
    def _():
        matrix = interleave()
        for part in range(2):
            image = jnp.concatenate([out[part, c] for c in range(COLS)], axis=1)
            image = permuted(image, matrix)
            for c in range(COLS):
                out[part, c] = image[:, lane_block(c)]


def fields_kernel(probe, kappa, out):
    matrix = interleave()
    for k in range(3):
        load_wrapped(out, (k,), permuted(probe[k] if k < 2 else kappa[...], matrix))


def frames_kernel(
    strip_index,
    partial,
    before,
    after,
    measured,
    wrapped,
    facts,
    out,
    known_out,
    window,
    local,
    field_a,
    field_b,
    field_c,
    total,
    positions,
):
    pad = 8
    known = facts[...]
    for frame in range(FRAMES):
        for k in range(2):
            place = measured[frame, 0, k : k + 1]
            positions[frame, k] = jnp.max(place).astype(jnp.int32)
            known = jnp.where(lane_ids(1) == 2 * frame + k, place, known)
    known_out[...] = jnp.broadcast_to(known, known_out.shape)
    window[...] = partial[:, :, SH - BASE : SH - BASE + ROWS]
    window[:, :, :SENT] += before[...]
    window[:, :, ROWS - SENT :] += after[...]
    total[...] = jnp.zeros_like(total)
    for field in (field_a, field_b, field_c):
        field[:, :, :pad] = jnp.zeros((2, COLS, pad, LANES), F32)
        field[:, :, pad + ROWS :] = jnp.zeros((2, COLS, pad, LANES), F32)
    tile = 16

    def laplace(field, part, row):
        centre = field[part, :, pl.ds(row, tile)]
        around = field[part, :, pl.ds(row - 1, tile)] + field[part, :, pl.ds(row + 1, tile)]
        left = jnp.concatenate([pltpu.roll(centre[COLS - 1 :], 1, 2), centre[: COLS - 1]], axis=0)
        right = jnp.concatenate([centre[1:], pltpu.roll(centre[:1], LANES - 1, 2)], axis=0)
        return centre, around + left + right - 4.0 * centre

    def per_frame(frame, _):
        first_row = (strip_index[0] * STRIP - BASE - positions[frame, 0]) & (NX - 1)
        for k in range(3):
            for c, block in enumerate(
                interleaved_roll(wrapped, (k,), first_row, ROWS, positions[frame, 1])
            ):
                local[k, c] = block
        tiles = range(0, ROWS, tile)
        for row in tiles:
            rows, padded = pl.ds(row, tile), pl.ds(row + pad, tile)
            probe_re, probe_im = local[0, :, rows], local[1, :, rows]
            re, im = window[0, :, rows], window[1, :, rows]
            field_a[0, :, padded] = probe_re * re - probe_im * im
            field_a[1, :, padded] = probe_re * im + probe_im * re
        for row in tiles:
            rows, padded = pl.ds(row, tile), pl.ds(row + pad, tile)
            re, lap_re = laplace(field_a, 0, row + pad)
            im, lap_im = laplace(field_a, 1, row + pad)
            kappa = local[2, :, rows]
            field_b[0, :, padded] = re - kappa * lap_im
            field_b[1, :, padded] = im + kappa * lap_re
        for row in tiles:
            rows, padded = pl.ds(row, tile), pl.ds(row + pad, tile)
            re, lap_re = laplace(field_b, 0, row + pad)
            im, lap_im = laplace(field_b, 1, row + pad)
            kappa = local[2, :, rows]
            wave_re = re - kappa * lap_im
            wave_im = im + kappa * lap_re
            twice = 2.0 * (wave_re * wave_re + wave_im * wave_im - measured[frame, :, rows])
            grad_re, grad_im = twice * wave_re, twice * wave_im
            field_a[0, :, padded] = grad_re
            field_a[1, :, padded] = grad_im
            field_c[0, :, padded] = kappa * grad_re
            field_c[1, :, padded] = kappa * grad_im
        for row in tiles:
            rows, padded = pl.ds(row, tile), pl.ds(row + pad, tile)
            _, lap_re = laplace(field_c, 0, row + pad)
            _, lap_im = laplace(field_c, 1, row + pad)
            kappa = local[2, :, rows]
            grad_re = field_a[0, :, padded] + lap_im
            grad_im = field_a[1, :, padded] - lap_re
            field_a[0, :, padded] = grad_re
            field_a[1, :, padded] = grad_im
            field_b[0, :, padded] = kappa * grad_re
            field_b[1, :, padded] = kappa * grad_im
        for row in range(0, STRIP, tile):
            rows, padded = pl.ds(row + BASE, tile), pl.ds(row + BASE + pad, tile)
            _, lap_re = laplace(field_b, 0, row + BASE + pad)
            _, lap_im = laplace(field_b, 1, row + BASE + pad)
            grad_re = field_a[0, :, padded] + lap_im
            grad_im = field_a[1, :, padded] - lap_re
            probe_re, probe_im = local[0, :, rows], local[1, :, rows]
            total[0, :, pl.ds(row, tile)] += probe_re * grad_re + probe_im * grad_im
            total[1, :, pl.ds(row, tile)] += probe_re * grad_im - probe_im * grad_re
        return 0

    lax.fori_loop(0, FRAMES, per_frame, 0)
    matrix = interleave(transposed=True)
    for part in range(2):
        image = jnp.concatenate([total[part, c] for c in range(COLS)], axis=1)
        image = permuted(image, matrix)
        for c in range(COLS):
            rows = pl.ds(part * COLS + c, STRIP, stride=BLOCKS)
            out[rows, :] = image[:, lane_block(c)]


def weight_kernel(strip_index, positions, probe, out, wrapped):
    load_wrapped(wrapped, (), probe[0] * probe[0] + probe[1] * probe[1])
    chunk = 32

    keeps = lane_ids(chunk)

    def per_angle(angle, _):
        firsts, wholes, parts = [], [], []
        for frame in range(FRAMES):
            top, amount = positions[angle, 2 * frame], positions[angle, 2 * frame + 1]
            firsts.append((strip_index[0] * STRIP - SH - top) & (NX - 1))
            wholes.append(amount >> 7)
            parts.append(amount & (LANES - 1))
        for row in range(0, RIM_ROWS, chunk):
            total = [jnp.zeros((chunk, LANES), F32)] * COLS
            for first, whole, part in zip(firsts, wholes, parts):
                turned = [
                    pltpu.roll(
                        wrapped[(c - whole) & (COLS - 1), pl.ds(first + row, chunk)], part, 1
                    )
                    for c in range(COLS)
                ]
                keep = keeps >= part
                total = [
                    total[c] + jnp.where(keep, turned[c], turned[c - 1]) for c in range(COLS)
                ]
            for c in range(COLS):
                out[angle, c, row : row + chunk] = total[c]
        return 0

    lax.fori_loop(0, ANGLES, per_angle, 0)


def divisor_kernel(shears, weights, out):
    base = pl.program_id(0) * out.shape[0]

    def per_slice(k, _):
        starts = [SH - shears[a, base + k] for a in range(ANGLES)]
        for c in range(COLS):
            total = jnp.ones((STRIP, LANES), F32)
            for a in range(ANGLES):
                total += weights[a, c, pl.ds(starts[a], STRIP)]
            out[k, :, lane_block(c)] = 1.0 / total
        return 0

    lax.fori_loop(0, out.shape[0], per_slice, 0)


def split(values):
    high = values.astype(BF16)
    return high, (values - high.astype(F32)).astype(BF16)


def pack_kernel(*refs):
    lasts, firsts, (last, first) = refs[:SIDE], refs[SIDE : 2 * SIDE], refs[2 * SIDE :]
    for k in range(SIDE):
        last[SIDE * k : SIDE * (k + 1)] = lasts[k][...]
        first[SIDE * k : SIDE * (k + 1)] = firsts[k][...]


def core_kernel(shears, own, two, one, three, slices, scale, out, grads, rows):
    @pl.when(pl.program_id(0) == 0)
    def _():
        for k, piece in enumerate((own, two, one, three)):
            grads[SIDE * k : SIDE * (k + 1), SH : SH + STRIP] = piece[...]
        grads[:, :SH] = jnp.zeros((ANGLES, SH, BLOCKS, LANES), F32)
        grads[:, SH + STRIP :] = jnp.zeros((ANGLES, SH, BLOCKS, LANES), F32)

    count = out.shape[0]
    base = pl.program_id(0) * count
    chunk = 16
    for k in range(count):
        starts = [SH - shears[a, base + k] for a in range(ANGLES)]
        for row in range(0, STRIP, chunk):
            total = grads[0, pl.ds(starts[0] + row, chunk)]
            for a in range(1, ANGLES):
                total += grads[a, pl.ds(starts[a] + row, chunk)]
            rows[k, row * BLOCKS : (row + chunk) * BLOCKS] = total.reshape(chunk * BLOCKS, LANES)
        for part in range(2):
            for c in range(COLS):
                total = rows[k, pl.ds(part * COLS + c, STRIP, stride=BLOCKS), :]
                cols = lane_block(c)
                out[k, part, :, cols] = slices[k, part, :, cols] - total * scale[k, :, cols]


def rim_kernel(shears, before, after, scale, core, out, high, low, shifts):
    side = pl.program_id(0)

    def take(rim):
        for a in range(ANGLES):
            for part in range(2):
                for c in range(COLS):
                    rows, cols = slice(a * SH, (a + 1) * SH), lane_block(part * COLS + c)
                    block = part * COLS + c
                    picked = pl.ds(a * SH * BLOCKS + block, SH, stride=BLOCKS)
                    high[rows, cols], low[rows, cols] = split(rim[picked, :])

    @pl.when((pl.program_id(1) == 0) & (side == 0))
    def _():
        take(before)

    @pl.when((pl.program_id(1) == 0) & (side == 1))
    def _():
        take(after)

    count = out.shape[0]
    width = ANGLES * SH
    column = lax.broadcasted_iota(jnp.int32, (SH, width), 1) & (SH - 1)
    apart = column - lax.broadcasted_iota(jnp.int32, (SH, width), 0)
    middle = jnp.where(side == 0, SH, -SH)
    for k in range(count):
        chosen = jnp.where(apart == middle - shears[k : k + 1], 1.0, 0.0)
        shifts[k * SH : (k + 1) * SH] = chosen.astype(BF16)
    product = jnp.dot(shifts[...], high[...], preferred_element_type=F32)
    product += jnp.dot(shifts[...], low[...], preferred_element_type=F32)
    for k in range(count):
        for part in range(2):
            total = product[k * SH : (k + 1) * SH, part * NY : (part + 1) * NY]
            out[k, part] = core[k, part] - total * scale[k]


def hop_pairs(hop, stage):
    pairs = []
    for y in range(SIDE):
        for x in range(SIDE):
            for block in range(FRAMES):
                along_x = (block % 2 == 0) == (stage == 0)
                to_y = y if along_x else (y + hop) % SIDE
                to_x = (x + hop) % SIDE if along_x else x
                pairs.append(((y * SIDE + x) * FRAMES + block, (to_y * SIDE + to_x) * FRAMES + block))
    return pairs


def gather_angles(grads, facts):
    axes = ("angle", "block")
    facts = lax.all_to_all(facts, "angle", 0, 0)[:, 0]
    row = jnp.stack([grads] + [lax.ppermute(grads, axes, hop_pairs(hop, 0)) for hop in HOPS])
    row, facts = lax.optimization_barrier((row, facts))
    pieces = [row] + [lax.ppermute(row, axes, hop_pairs(hop, 1)) for hop in HOPS]
    angle = lax.axis_index("angle")
    odd = lax.axis_index("block") % 2
    first, second = jnp.asarray((0,) + HOPS), jnp.asarray((0,) + HOPS)
    along_x = jnp.where(odd == 1, second[:, None], first[None])
    along_y = jnp.where(odd == 1, first[None], second[:, None])
    order = ((angle // SIDE - along_y) % SIDE) * SIDE + (angle - along_x) % SIDE
    return pieces, order.reshape(ANGLES), facts.astype(jnp.int32)


def per_device(object_field, shears, positions, measured, probe_field, kappa_field):
    strip_index = lax.axis_index("block").astype(jnp.int32)[None]
    moved = pl.pallas_call(
        measured_kernel,
        out_shape=jax.ShapeDtypeStruct((FRAMES, COLS, ROWS, LANES), F32),
        in_specs=[SMEM, VMEM],
        out_specs=VMEM,
        scratch_shapes=[pltpu.VMEM((COLS, WRAP, LANES), F32)],
        compiler_params=vmem(60),
        cost_estimate=cost(3),
        name="measured_rows",
    )(positions[0, 0], measured[0, 0])
    observed = lax.all_to_all(moved, "block", 0, 0)
    step = 4
    partial = pl.pallas_call(
        project_kernel,
        grid=(Z // step,),
        out_shape=jax.ShapeDtypeStruct((2, COLS, RIM_ROWS, LANES), F32),
        in_specs=[SMEM, pl.BlockSpec((step, 2, STRIP, NY), lambda i: (i, 0, 0, 0))],
        out_specs=pl.BlockSpec((2, COLS, RIM_ROWS, LANES), lambda i: (0, 0, 0, 0)),
        compiler_params=vmem(60),
        cost_estimate=cost(7),
        name="project",
    )(shears[0], object_field)
    count = FRAMES
    up = [(i, (i + 1) % count) for i in range(count)]
    down = [(j, i) for i, j in up]
    before = lax.ppermute(partial[:, :, RIM_ROWS - SENT :], "block", up)
    after = lax.ppermute(partial[:, :, :SENT], "block", down)
    wrapped = pl.pallas_call(
        fields_kernel,
        out_shape=jax.ShapeDtypeStruct((3, COLS, WRAP, LANES), F32),
        in_specs=[VMEM, VMEM],
        out_specs=VMEM,
        compiler_params=vmem(60),
        cost_estimate=cost(6),
        name="fields",
    )(probe_field, kappa_field[0])

    facts = jnp.pad(shears.astype(F32), ((0, 0), (2 * FRAMES, LANES - 2 * FRAMES - Z)))
    field = pltpu.VMEM((2, COLS, ROWS + 16, LANES), F32)
    grads, facts = pl.pallas_call(
        frames_kernel,
        out_shape=[
            jax.ShapeDtypeStruct((STRIP * BLOCKS, LANES), F32),
            jax.ShapeDtypeStruct((ANGLES * 8, LANES), F32),
        ],
        in_specs=[SMEM] + [VMEM] * 6,
        out_specs=[VMEM, VMEM],
        scratch_shapes=[
            pltpu.VMEM((2, COLS, ROWS, LANES), F32),
            pltpu.VMEM((3, COLS, ROWS, LANES), F32),
            field,
            field,
            field,
            pltpu.VMEM((2, COLS, STRIP, LANES), F32),
            pltpu.SMEM((FRAMES, 2), jnp.int32),
        ],
        compiler_params=vmem(15),
        cost_estimate=cost(9),
        name="frames",
    )(strip_index, partial, before, after, observed, wrapped, facts)
    pieces, order, facts = gather_angles(
        grads.reshape(STRIP, BLOCKS, LANES), facts.reshape(ANGLES, 8, LANES)
    )
    facts = jnp.take(facts, order, axis=0)
    all_positions = facts[:, : 2 * FRAMES]
    all_shears = facts[:, 2 * FRAMES : 2 * FRAMES + Z]
    rim_shears = all_shears.reshape(SIDE, SIDE, Z).transpose(2, 1, 0).reshape(Z, ANGLES)
    rim_shears = jnp.repeat(rim_shears, SH, axis=1)

    weights = pl.pallas_call(
        weight_kernel,
        out_shape=jax.ShapeDtypeStruct((ANGLES, COLS, RIM_ROWS, LANES), F32),
        in_specs=[SMEM, SMEM, VMEM],
        out_specs=VMEM,
        scratch_shapes=[pltpu.VMEM((COLS, WRAP, LANES), F32)],
        compiler_params=vmem(12),
        cost_estimate=cost(2),
        name="weights",
    )(strip_index, all_positions, probe_field)
    slices_spec = pl.BlockSpec((step, STRIP, NY), lambda i: (i, 0, 0))
    scale = pl.pallas_call(
        divisor_kernel,
        grid=(Z // step,),
        out_shape=jax.ShapeDtypeStruct((Z, STRIP, NY), F32),
        in_specs=[SMEM, VMEM],
        out_specs=slices_spec,
        compiler_params=vmem(8),
        cost_estimate=cost(2),
        name="divisor",
    )(all_shears, weights)

    scale, rim_shears, *pieces = lax.optimization_barrier((scale, rim_shears, *pieces))
    edge = (SIDE, SH, BLOCKS, LANES)
    rims = pl.pallas_call(
        pack_kernel,
        grid=(1,),
        out_shape=[jax.ShapeDtypeStruct((ANGLES, SH, BLOCKS, LANES), F32)] * 2,
        in_specs=[pl.BlockSpec(edge, lambda i: (0, STRIP // SH - 1, 0, 0))] * SIDE
        + [pl.BlockSpec(edge, lambda i: (0, 0, 0, 0))] * SIDE,
        out_specs=[pl.BlockSpec((ANGLES, SH, BLOCKS, LANES), lambda i: (0, 0, 0, 0))] * 2,
        compiler_params=vmem(12),
        cost_estimate=cost(2),
        name="pack",
    )(*pieces, *pieces)
    rims = [
        lax.ppermute(rim, "block", pairs).reshape(ANGLES * SH * BLOCKS, LANES)
        for rim, pairs in zip(rims, (up, down))
    ]

    object_spec = pl.BlockSpec((step, 2, STRIP, NY), lambda i: (i, 0, 0, 0))
    core = pl.pallas_call(
        core_kernel,
        grid=(Z // step,),
        out_shape=jax.ShapeDtypeStruct(object_field.shape, F32),
        in_specs=[SMEM] + [VMEM] * 4 + [object_spec, slices_spec],
        out_specs=object_spec,
        scratch_shapes=[
            pltpu.VMEM((ANGLES, RIM_ROWS, BLOCKS, LANES), F32),
            pltpu.VMEM((step, STRIP * BLOCKS, LANES), F32),
        ],
        compiler_params=vmem(50),
        cost_estimate=cost(17),
        name="core",
    )(all_shears, *pieces, object_field, scale)
    many = 16
    edge_spec = pl.BlockSpec((many, 2, SH, NY), lambda j, i: (i, 0, j * (STRIP // SH - 1), 0))
    return pl.pallas_call(
        rim_kernel,
        grid=(2, Z // many),
        out_shape=jax.ShapeDtypeStruct(object_field.shape, F32),
        in_specs=[pl.BlockSpec((many, ANGLES * SH), lambda j, i: (i, 0)), VMEM, VMEM]
        + [pl.BlockSpec((many, SH, NY), lambda j, i: (i, j * (STRIP // SH - 1), 0)), edge_spec],
        out_specs=edge_spec,
        scratch_shapes=[
            pltpu.VMEM((ANGLES * SH, 2 * NY), BF16),
            pltpu.VMEM((ANGLES * SH, 2 * NY), BF16),
            pltpu.VMEM((many * SH, ANGLES * SH), BF16),
        ],
        input_output_aliases={4: 0},
        compiler_params=vmem(50),
        cost_estimate=cost(9),
        name="rim",
    )(rim_shears, *rims, scale, core)


def solution(mesh):
    placed = (
        P(None, None, "block", None),
        P("angle", None),
        P("angle", "block", None),
        P("angle", "block", None, None),
        P(),
        P("angle", None, None),
    )
    return jax.shard_map(
        per_device,
        mesh=mesh,
        in_specs=placed,
        out_specs=P(None, None, "block", None),
        check_vma=False,
    )
```

```python
import jax
import jax.numpy as jnp
from jax import lax
from jax.experimental import pallas as pl
from jax.experimental.pallas import tpu as pltpu
from jax.sharding import PartitionSpec as P

NX = 512
NY = 512
Z = 32
SH = 16
ANGLES = 16
FRAMES = 8
STRIP = 64
LANES = 128
COLS = NY // LANES
BASE = 8
ROWS = STRIP + 2 * BASE
RIM_ROWS = STRIP + 2 * SH
SENT = BASE + SH
WRAP = NX + RIM_ROWS
F32 = jnp.float32
BF16 = jnp.bfloat16
HOPS = (2, 1, 3)
SIDE = 4
SPARE = 16
BLOCKS = 2 * COLS
COST_SCALE = 3_000_000

SMEM = pl.BlockSpec(memory_space=pltpu.SMEM)
VMEM = pl.BlockSpec(memory_space=pltpu.VMEM)


def cost(microseconds):
    return pl.CostEstimate(
        flops=0, transcendentals=0, bytes_accessed=microseconds * COST_SCALE
    )


def vmem(mebibytes):
    return pltpu.CompilerParams(vmem_limit_bytes=mebibytes * 2**20)


def lane_block(c):
    return slice(c * LANES, (c + 1) * LANES)


def lane_ids(rows):
    return lax.broadcasted_iota(jnp.int32, (rows, LANES), 1)


def load_wrapped(scratch, index, image):
    for c in range(COLS):
        scratch[index + (c, pl.ds(0, NX))] = image[:, lane_block(c)]
        scratch[index + (c, pl.ds(NX, WRAP - NX))] = image[: WRAP - NX, lane_block(c)]


def interleave(transposed=False):
    old = lax.broadcasted_iota(jnp.int32, (NY, NY), 1 if transposed else 0)
    new = lax.broadcasted_iota(jnp.int32, (NY, NY), 0 if transposed else 1)
    return jnp.where(old == (new % LANES) * COLS + new // LANES, 1.0, 0.0).astype(BF16)


def permuted(image, matrix):
    result = None
    for term in range(3):
        high = image.astype(BF16)
        product = jnp.dot(high, matrix, preferred_element_type=F32)
        result = product if result is None else result + product
        if term < 2:
            image = image - high.astype(F32)
    return result


def interleaved_roll(scratch, index, first_row, rows, amount):
    whole, part = amount >> 2, amount & (COLS - 1)
    return [
        pltpu.roll(
            scratch[index + ((c - part) & (COLS - 1), pl.ds(first_row, rows))],
            (whole + jnp.where(c < part, 1, 0)) & (LANES - 1),
            1,
        )
        for c in range(COLS)
    ]


def measured_kernel(position, measured, out, wrapped):
    load_wrapped(
        wrapped, (), jnp.dot(measured[...], interleave(), preferred_element_type=F32)
    )
    for strip in range(FRAMES):
        first_row = (strip * STRIP - BASE - position[0]) & (NX - 1)
        for c, block in enumerate(interleaved_roll(wrapped, (), first_row, ROWS, position[1])):
            out[strip, c] = block
        for k in range(2):
            out[strip, 0, k : k + 1] = jnp.full((1, LANES), position[k].astype(F32), F32)


def project_kernel(shears, slices, out):
    step = pl.program_id(0)

    @pl.when(step == 0)
    def _():
        out[...] = jnp.zeros_like(out)

    count = slices.shape[0]
    for k in range(count):
        rows = pl.ds(SH - shears[step * count + k], STRIP)
        for part in range(2):
            for c in range(COLS):
                out[part, c, rows] += slices[k, part, :, lane_block(c)]

    @pl.when(step == pl.num_programs(0) - 1)
    def _():
        matrix = interleave()
        for part in range(2):
            image = jnp.concatenate([out[part, c] for c in range(COLS)], axis=1)
            image = permuted(image, matrix)
            for c in range(COLS):
                out[part, c] = image[:, lane_block(c)]


def fields_kernel(probe, kappa, out):
    matrix = interleave()
    for k in range(3):
        load_wrapped(out, (k,), permuted(probe[k] if k < 2 else kappa[...], matrix))


def frames_kernel(
    strip_index,
    partial,
    before,
    after,
    measured,
    fields,
    facts,
    out,
    known_out,
    wrapped,
    arrival,
    window,
    local,
    field_a,
    field_b,
    field_c,
    total,
    positions,
):
    pad = 8
    copy = pltpu.make_async_copy(fields.at[pl.ds(0, 3)], wrapped, arrival)
    copy.start()
    known = facts[...]
    for frame in range(FRAMES):
        for k in range(2):
            place = measured[frame, 0, k : k + 1]
            positions[frame, k] = jnp.max(place).astype(jnp.int32)
            known = jnp.where(lane_ids(1) == 2 * frame + k, place, known)
    known_out[...] = jnp.broadcast_to(known, known_out.shape)
    window[...] = partial[:, :, SH - BASE : SH - BASE + ROWS]
    window[:, :, :SENT] += before[...]
    window[:, :, ROWS - SENT :] += after[...]
    total[...] = jnp.zeros_like(total)
    for field in (field_a, field_b, field_c):
        field[:, :, :pad] = jnp.zeros((2, COLS, pad, LANES), F32)
        field[:, :, pad + ROWS :] = jnp.zeros((2, COLS, pad, LANES), F32)
    tile = 16

    def laplace(field, part, row):
        centre = field[part, :, pl.ds(row, tile)]
        around = field[part, :, pl.ds(row - 1, tile)] + field[part, :, pl.ds(row + 1, tile)]
        left = jnp.concatenate([pltpu.roll(centre[COLS - 1 :], 1, 2), centre[: COLS - 1]], axis=0)
        right = jnp.concatenate([centre[1:], pltpu.roll(centre[:1], LANES - 1, 2)], axis=0)
        return centre, around + left + right - 4.0 * centre

    def per_frame(frame, _):
        first_row = (strip_index[0] * STRIP - BASE - positions[frame, 0]) & (NX - 1)
        for k in range(3):
            for c, block in enumerate(
                interleaved_roll(wrapped, (k,), first_row, ROWS, positions[frame, 1])
            ):
                local[k, c] = block
        tiles = range(0, ROWS, tile)
        for row in tiles:
            rows, padded = pl.ds(row, tile), pl.ds(row + pad, tile)
            probe_re, probe_im = local[0, :, rows], local[1, :, rows]
            re, im = window[0, :, rows], window[1, :, rows]
            field_a[0, :, padded] = probe_re * re - probe_im * im
            field_a[1, :, padded] = probe_re * im + probe_im * re
        for row in tiles:
            rows, padded = pl.ds(row, tile), pl.ds(row + pad, tile)
            re, lap_re = laplace(field_a, 0, row + pad)
            im, lap_im = laplace(field_a, 1, row + pad)
            kappa = local[2, :, rows]
            field_b[0, :, padded] = re - kappa * lap_im
            field_b[1, :, padded] = im + kappa * lap_re
        for row in tiles:
            rows, padded = pl.ds(row, tile), pl.ds(row + pad, tile)
            re, lap_re = laplace(field_b, 0, row + pad)
            im, lap_im = laplace(field_b, 1, row + pad)
            kappa = local[2, :, rows]
            wave_re = re - kappa * lap_im
            wave_im = im + kappa * lap_re
            twice = 2.0 * (wave_re * wave_re + wave_im * wave_im - measured[frame, :, rows])
            grad_re, grad_im = twice * wave_re, twice * wave_im
            field_a[0, :, padded] = grad_re
            field_a[1, :, padded] = grad_im
            field_c[0, :, padded] = kappa * grad_re
            field_c[1, :, padded] = kappa * grad_im
        for row in tiles:
            rows, padded = pl.ds(row, tile), pl.ds(row + pad, tile)
            _, lap_re = laplace(field_c, 0, row + pad)
            _, lap_im = laplace(field_c, 1, row + pad)
            kappa = local[2, :, rows]
            grad_re = field_a[0, :, padded] + lap_im
            grad_im = field_a[1, :, padded] - lap_re
            field_a[0, :, padded] = grad_re
            field_a[1, :, padded] = grad_im
            field_b[0, :, padded] = kappa * grad_re
            field_b[1, :, padded] = kappa * grad_im
        for row in range(0, STRIP, tile):
            rows, padded = pl.ds(row + BASE, tile), pl.ds(row + BASE + pad, tile)
            _, lap_re = laplace(field_b, 0, row + BASE + pad)
            _, lap_im = laplace(field_b, 1, row + BASE + pad)
            grad_re = field_a[0, :, padded] + lap_im
            grad_im = field_a[1, :, padded] - lap_re
            probe_re, probe_im = local[0, :, rows], local[1, :, rows]
            total[0, :, pl.ds(row, tile)] += probe_re * grad_re + probe_im * grad_im
            total[1, :, pl.ds(row, tile)] += probe_re * grad_im - probe_im * grad_re
        return 0

    copy.wait()
    lax.fori_loop(0, FRAMES, per_frame, 0)
    matrix = interleave(transposed=True)
    for part in range(2):
        image = jnp.concatenate([total[part, c] for c in range(COLS)], axis=1)
        image = permuted(image, matrix)
        for c in range(COLS):
            rows = pl.ds(part * COLS + c, STRIP, stride=BLOCKS)
            out[rows, :] = image[:, lane_block(c)]


def gather_weights(strip_index, positions, probe, out, wrapped):
    load_wrapped(wrapped, (), probe[0] * probe[0] + probe[1] * probe[1])
    chunk = 32

    keeps = lane_ids(chunk)

    def per_angle(angle, _):
        firsts, wholes, parts = [], [], []
        for frame in range(FRAMES):
            top, amount = positions[angle, 2 * frame], positions[angle, 2 * frame + 1]
            firsts.append((strip_index[0] * STRIP - SH - top) & (NX - 1))
            wholes.append(amount >> 7)
            parts.append(amount & (LANES - 1))
        for row in range(0, RIM_ROWS, chunk):
            total = [jnp.zeros((chunk, LANES), F32)] * COLS
            for first, whole, part in zip(firsts, wholes, parts):
                turned = [
                    pltpu.roll(
                        wrapped[(c - whole) & (COLS - 1), pl.ds(first + row, chunk)], part, 1
                    )
                    for c in range(COLS)
                ]
                keep = keeps >= part
                total = [
                    total[c] + jnp.where(keep, turned[c], turned[c - 1]) for c in range(COLS)
                ]
            for c in range(COLS):
                out[angle, c, row : row + chunk] = total[c]
        return 0

    lax.fori_loop(0, ANGLES, per_angle, 0)


def divisor_kernel(
    strip_index,
    positions,
    shears,
    probe,
    own,
    slices,
    out,
    rest,
    weights,
    wrapped,
    grads,
    rows,
):
    @pl.when(pl.program_id(0) == 0)
    def _():
        gather_weights(strip_index, positions, probe, weights, wrapped)
        fill_grads(grads, (own,))

    base = pl.program_id(0) * out.shape[0]

    def per_slice(k, _):
        starts = [SH - shears[a, base + k] for a in range(ANGLES)]
        for c in range(COLS):
            total = jnp.ones((STRIP, LANES), F32)
            for a in range(ANGLES):
                total += weights[a, c, pl.ds(starts[a], STRIP)]
            out[k, :, lane_block(c)] = 1.0 / total
        take_grads(starts[:SIDE], grads, rows, slices.at[k], out.at[k], rest.at[k])
        return 0

    lax.fori_loop(0, out.shape[0], per_slice, 0)


def split(values):
    high = values.astype(BF16)
    return high, (values - high.astype(F32)).astype(BF16)


def pack_kernel(*refs):
    last, first = refs[-2:]
    for k in range(2):

        @pl.when(pl.program_id(0) == k)
        def _():
            last[...] = refs[2 * k][...]
            first[...] = refs[2 * k + 1][...]


def pack(pieces, places, rims):
    edge = (SIDE, SH, BLOCKS, LANES)
    ends = [
        pl.BlockSpec(edge, lambda i: (0, STRIP // SH - 1, 0, 0)),
        pl.BlockSpec(edge, lambda i: (0, 0, 0, 0)),
    ]
    start, stride = places[0], places[1] - places[0]
    return pl.pallas_call(
        pack_kernel,
        grid=(2,),
        out_shape=[jax.ShapeDtypeStruct((ANGLES, SH, BLOCKS, LANES), F32)] * 2,
        in_specs=ends * 2 + [pl.BlockSpec(memory_space=pl.ANY)] * len(rims),
        out_specs=[pl.BlockSpec(edge, lambda i: (start + i * stride, 0, 0, 0))] * 2,
        input_output_aliases={4 + k: k for k in range(len(rims))},
        compiler_params=vmem(12),
        cost_estimate=cost(1),
        name="pack",
    )(pieces[0], pieces[0], pieces[1], pieces[1], *rims)


def fill_grads(grads, pieces):
    for k, piece in enumerate(pieces):
        grads[SIDE * k : SIDE * (k + 1), SH : SH + STRIP] = piece[...]
    count = SIDE * len(pieces)
    grads[:, :SH] = jnp.zeros((count, SH, BLOCKS, LANES), F32)
    grads[:, SH + STRIP :] = jnp.zeros((count, SH, BLOCKS, LANES), F32)


def take_grads(starts, grads, rows, slices, scale, out):
    chunk = 8
    for row in range(0, STRIP, chunk):
        total = grads[0, pl.ds(starts[0] + row, chunk)]
        for a in range(1, len(starts)):
            total += grads[a, pl.ds(starts[a] + row, chunk)]
        rows[row * BLOCKS : (row + chunk) * BLOCKS] = total.reshape(chunk * BLOCKS, LANES)
    for part in range(2):
        for c in range(COLS):
            total = rows[pl.ds(part * COLS + c, STRIP, stride=BLOCKS), :]
            cols = lane_block(c)
            out[part, :, cols] = slices[part, :, cols] - total * scale[:, cols]


def core_kernel(shears, two, one, three, slices, scale, out, grads, rows):
    @pl.when(pl.program_id(0) == 0)
    def _():
        fill_grads(grads, (two, one, three))

    count = out.shape[0]
    base = pl.program_id(0) * count
    for k in range(count):
        starts = [SH - shears[a, base + k] for a in range(SIDE, ANGLES)]
        take_grads(
            starts, grads, rows.at[k], slices.at[k], scale.at[k], out.at[k]
        )


def rim_kernel(shears, before, after, scale, core, out, high, low, shifts):
    side = pl.program_id(0)

    def take(rim):
        for a in range(ANGLES):
            for part in range(2):
                for c in range(COLS):
                    rows, cols = slice(a * SH, (a + 1) * SH), lane_block(part * COLS + c)
                    block = part * COLS + c
                    picked = pl.ds(a * SH * BLOCKS + block, SH, stride=BLOCKS)
                    high[rows, cols], low[rows, cols] = split(rim[picked, :])

    @pl.when((pl.program_id(1) == 0) & (side == 0))
    def _():
        take(before)

    @pl.when((pl.program_id(1) == 0) & (side == 1))
    def _():
        take(after)

    count = out.shape[0]
    width = ANGLES * SH
    column = lax.broadcasted_iota(jnp.int32, (SH, width), 1) & (SH - 1)
    apart = column - lax.broadcasted_iota(jnp.int32, (SH, width), 0)
    middle = jnp.where(side == 0, SH, -SH)
    for k in range(count):
        chosen = jnp.where(apart == middle - shears[k : k + 1], 1.0, 0.0)
        shifts[k * SH : (k + 1) * SH] = chosen.astype(BF16)
    product = jnp.dot(shifts[...], high[...], preferred_element_type=F32)
    product += jnp.dot(shifts[...], low[...], preferred_element_type=F32)
    for k in range(count):
        for part in range(2):
            total = product[k * SH : (k + 1) * SH, part * NY : (part + 1) * NY]
            out[k, part] = core[k, part] - total * scale[k]


def hop_pairs(hop, stage):
    pairs = []
    for y in range(SIDE):
        for x in range(SIDE):
            for block in range(FRAMES):
                along_x = (block % 2 == 0) == (stage == 0)
                to_y = y if along_x else (y + hop) % SIDE
                to_x = (x + hop) % SIDE if along_x else x
                pairs.append(((y * SIDE + x) * FRAMES + block, (to_y * SIDE + to_x) * FRAMES + block))
    return pairs


def gather_angles(grads, facts):
    axes = ("angle", "block")
    facts = lax.all_to_all(facts, "angle", 0, 0)[:, 0]
    row = jnp.stack([grads] + [lax.ppermute(grads, axes, hop_pairs(hop, 0)) for hop in HOPS])
    row, facts = lax.optimization_barrier((row, facts))
    pieces = [row] + [lax.ppermute(row, axes, hop_pairs(hop, 1)) for hop in HOPS]
    angle = lax.axis_index("angle")
    odd = lax.axis_index("block") % 2
    first, second = jnp.asarray((0,) + HOPS), jnp.asarray((0,) + HOPS)
    along_x = jnp.where(odd == 1, second[:, None], first[None])
    along_y = jnp.where(odd == 1, first[None], second[:, None])
    order = ((angle // SIDE - along_y) % SIDE) * SIDE + (angle - along_x) % SIDE
    return pieces, order.reshape(ANGLES), facts.astype(jnp.int32)


def per_device(object_field, shears, positions, measured, probe_field, kappa_field):
    strip_index = lax.axis_index("block").astype(jnp.int32)[None]
    moved = pl.pallas_call(
        measured_kernel,
        out_shape=jax.ShapeDtypeStruct((FRAMES, COLS, ROWS, LANES), F32),
        in_specs=[SMEM, VMEM],
        out_specs=VMEM,
        scratch_shapes=[pltpu.VMEM((COLS, WRAP, LANES), F32)],
        compiler_params=vmem(60),
        cost_estimate=cost(3),
        name="measured_rows",
    )(positions[0, 0], measured[0, 0])
    observed = lax.all_to_all(moved, "block", 0, 0)
    step = 4
    partial = pl.pallas_call(
        project_kernel,
        grid=(Z // step,),
        out_shape=jax.ShapeDtypeStruct((2, COLS, RIM_ROWS, LANES), F32),
        in_specs=[SMEM, pl.BlockSpec((step, 2, STRIP, NY), lambda i: (i, 0, 0, 0))],
        out_specs=pl.BlockSpec((2, COLS, RIM_ROWS, LANES), lambda i: (0, 0, 0, 0)),
        compiler_params=vmem(60),
        cost_estimate=cost(7),
        name="project",
    )(shears[0], object_field)
    count = FRAMES
    up = [(i, (i + 1) % count) for i in range(count)]
    down = [(j, i) for i, j in up]
    before = lax.ppermute(partial[:, :, RIM_ROWS - SENT :], "block", up)
    after = lax.ppermute(partial[:, :, :SENT], "block", down)
    wrapped = pl.pallas_call(
        fields_kernel,
        grid=(1,),
        out_shape=jax.ShapeDtypeStruct((3 * SPARE, COLS, WRAP, LANES), F32),
        in_specs=[VMEM, VMEM],
        out_specs=pl.BlockSpec((3, COLS, WRAP, LANES), lambda i: (0, 0, 0, 0)),
        compiler_params=vmem(60),
        cost_estimate=cost(6),
        name="fields",
    )(probe_field, kappa_field[0])

    facts = jnp.pad(shears.astype(F32), ((0, 0), (2 * FRAMES, LANES - 2 * FRAMES - Z)))
    field = pltpu.VMEM((2, COLS, ROWS + 16, LANES), F32)
    grads, facts = pl.pallas_call(
        frames_kernel,
        out_shape=[
            jax.ShapeDtypeStruct((STRIP * BLOCKS, LANES), F32),
            jax.ShapeDtypeStruct((ANGLES * 8, LANES), F32),
        ],
        in_specs=[SMEM] + [VMEM] * 4 + [pl.BlockSpec(memory_space=pltpu.HBM), VMEM],
        out_specs=[VMEM, VMEM],
        scratch_shapes=[
            pltpu.VMEM((3, COLS, WRAP, LANES), F32),
            pltpu.SemaphoreType.DMA,
            pltpu.VMEM((2, COLS, ROWS, LANES), F32),
            pltpu.VMEM((3, COLS, ROWS, LANES), F32),
            field,
            field,
            field,
            pltpu.VMEM((2, COLS, STRIP, LANES), F32),
            pltpu.SMEM((FRAMES, 2), jnp.int32),
        ],
        compiler_params=vmem(15),
        cost_estimate=cost(9),
        name="frames",
    )(strip_index, partial, before, after, observed, wrapped, facts)
    pieces, order, facts = gather_angles(
        grads.reshape(STRIP, BLOCKS, LANES), facts.reshape(ANGLES, 8, LANES)
    )
    facts = jnp.take(facts, order, axis=0)
    all_positions = facts[:, : 2 * FRAMES]
    all_shears = facts[:, 2 * FRAMES : 2 * FRAMES + Z]
    rim_shears = all_shears.reshape(SIDE, SIDE, Z).transpose(2, 1, 0).reshape(Z, ANGLES)
    rim_shears = jnp.repeat(rim_shears, SH, axis=1)

    slices_spec = pl.BlockSpec((step, STRIP, NY), lambda i: (i, 0, 0))
    own, two, one, three = pieces
    object_spec = pl.BlockSpec((step, 2, STRIP, NY), lambda i: (i, 0, 0, 0))
    scale, rest = pl.pallas_call(
        divisor_kernel,
        grid=(Z // step,),
        out_shape=[
            jax.ShapeDtypeStruct((Z, STRIP, NY), F32),
            jax.ShapeDtypeStruct(object_field.shape, F32),
        ],
        in_specs=[SMEM, SMEM, SMEM, VMEM, VMEM, object_spec],
        out_specs=[slices_spec, object_spec],
        scratch_shapes=[
            pltpu.VMEM((ANGLES, COLS, RIM_ROWS, LANES), F32),
            pltpu.VMEM((COLS, WRAP, LANES), F32),
            pltpu.VMEM((SIDE, RIM_ROWS, BLOCKS, LANES), F32),
            pltpu.VMEM((STRIP * BLOCKS, LANES), F32),
        ],
        compiler_params=vmem(60),
        cost_estimate=cost(2),
        name="divisor",
    )(strip_index, all_positions, all_shears, probe_field, own, object_field)

    scale, rim_shears, own, three = lax.optimization_barrier((scale, rim_shears, own, three))
    rims = pack((own, three), (0, 3), ())
    rims = pack((two, one), (1, 2), rims)
    pieces = (two, one, three)
    rims = [
        lax.ppermute(rim, "block", pairs).reshape(ANGLES * SH * BLOCKS, LANES)
        for rim, pairs in zip(rims, (up, down))
    ]

    step = 8
    slices_spec = pl.BlockSpec((step, STRIP, NY), lambda i: (i, 0, 0))
    object_spec = pl.BlockSpec((step, 2, STRIP, NY), lambda i: (i, 0, 0, 0))
    core = pl.pallas_call(
        core_kernel,
        grid=(Z // step,),
        out_shape=jax.ShapeDtypeStruct(object_field.shape, F32),
        in_specs=[SMEM] + [VMEM] * 3 + [object_spec, slices_spec],
        out_specs=object_spec,
        scratch_shapes=[
            pltpu.VMEM((ANGLES - SIDE, RIM_ROWS, BLOCKS, LANES), F32),
            pltpu.VMEM((step, STRIP * BLOCKS, LANES), F32),
        ],
        compiler_params=vmem(50),
        cost_estimate=cost(17),
        name="core",
    )(all_shears, *pieces, rest, scale)
    many = 32
    edge_spec = pl.BlockSpec((many, 2, SH, NY), lambda j, i: (i, 0, j * (STRIP // SH - 1), 0))
    return pl.pallas_call(
        rim_kernel,
        grid=(2, Z // many),
        out_shape=jax.ShapeDtypeStruct(object_field.shape, F32),
        in_specs=[pl.BlockSpec((many, ANGLES * SH), lambda j, i: (i, 0)), VMEM, VMEM]
        + [pl.BlockSpec((many, SH, NY), lambda j, i: (i, j * (STRIP // SH - 1), 0)), edge_spec],
        out_specs=edge_spec,
        scratch_shapes=[
            pltpu.VMEM((ANGLES * SH, 2 * NY), BF16),
            pltpu.VMEM((ANGLES * SH, 2 * NY), BF16),
            pltpu.VMEM((many * SH, ANGLES * SH), BF16),
        ],
        input_output_aliases={4: 0},
        compiler_params=vmem(50),
        cost_estimate=cost(9),
        name="rim",
    )(rim_shears, *rims, scale, core)


def solution(mesh):
    placed = (
        P(None, None, "block", None),
        P("angle", None),
        P("angle", "block", None),
        P("angle", "block", None, None),
        P(),
        P("angle", None, None),
    )
    return jax.shard_map(
        per_device,
        mesh=mesh,
        in_specs=placed,
        out_specs=P(None, None, "block", None),
        check_vma=False,
    )
```

```python
import jax
import jax.numpy as jnp
from jax import lax
from jax.experimental import pallas as pl
from jax.experimental.pallas import tpu as pltpu
from jax.sharding import PartitionSpec as P

NX = 512
NY = 512
Z = 32
SH = 16
ANGLES = 16
FRAMES = 8
STRIP = 64
LANES = 128
COLS = NY // LANES
BASE = 8
ROWS = STRIP + 2 * BASE
SEEN_BASE = 4
SEEN_ROWS = STRIP + 2 * SEEN_BASE
RIM_ROWS = STRIP + 2 * SH
SENT = BASE + SH
WRAP = NX + RIM_ROWS
F32 = jnp.float32
BF16 = jnp.bfloat16
HOPS = (2, 1, 3)
SIDE = 4
SPARE = 16
BLOCKS = 2 * COLS
COST_SCALE = 3_000_000

SMEM = pl.BlockSpec(memory_space=pltpu.SMEM)
VMEM = pl.BlockSpec(memory_space=pltpu.VMEM)


def cost(microseconds):
    return pl.CostEstimate(
        flops=0, transcendentals=0, bytes_accessed=microseconds * COST_SCALE
    )


def vmem(mebibytes):
    return pltpu.CompilerParams(vmem_limit_bytes=mebibytes * 2**20)


def lane_block(c):
    return slice(c * LANES, (c + 1) * LANES)


def lane_ids(rows):
    return lax.broadcasted_iota(jnp.int32, (rows, LANES), 1)


def load_wrapped(scratch, index, image):
    for c in range(COLS):
        scratch[index + (c, pl.ds(0, NX))] = image[:, lane_block(c)]
        scratch[index + (c, pl.ds(NX, WRAP - NX))] = image[: WRAP - NX, lane_block(c)]


def interleave(transposed=False):
    old = lax.broadcasted_iota(jnp.int32, (NY, NY), 1 if transposed else 0)
    new = lax.broadcasted_iota(jnp.int32, (NY, NY), 0 if transposed else 1)
    return jnp.where(old == (new % LANES) * COLS + new // LANES, 1.0, 0.0).astype(BF16)


def permuted(image, matrix):
    result = None
    for term in range(3):
        high = image.astype(BF16)
        product = jnp.dot(high, matrix, preferred_element_type=F32)
        result = product if result is None else result + product
        if term < 2:
            image = image - high.astype(F32)
    return result


def interleaved_roll(scratch, index, first_row, rows, amount):
    whole, part = amount >> 2, amount & (COLS - 1)
    return [
        pltpu.roll(
            scratch[index + ((c - part) & (COLS - 1), pl.ds(first_row, rows))],
            (whole + jnp.where(c < part, 1, 0)) & (LANES - 1),
            1,
        )
        for c in range(COLS)
    ]


def measured_kernel(position, measured, out, wrapped):
    load_wrapped(
        wrapped, (), jnp.dot(measured[...], interleave(), preferred_element_type=F32)
    )
    for strip in range(FRAMES):
        first_row = (strip * STRIP - SEEN_BASE - position[0]) & (NX - 1)
        for c, block in enumerate(interleaved_roll(wrapped, (), first_row, SEEN_ROWS, position[1])):
            out[strip, c] = block
        for k in range(2):
            out[strip, 0, k : k + 1] = jnp.full((1, LANES), position[k].astype(F32), F32)


def project_kernel(shears, slices, out):
    step = pl.program_id(0)

    @pl.when(step == 0)
    def _():
        out[...] = jnp.zeros_like(out)

    count = slices.shape[0]
    for k in range(count):
        rows = pl.ds(SH - shears[step * count + k], STRIP)
        for part in range(2):
            for c in range(COLS):
                out[part, c, rows] += slices[k, part, :, lane_block(c)]

    @pl.when(step == pl.num_programs(0) - 1)
    def _():
        matrix = interleave()
        for part in range(2):
            image = jnp.concatenate([out[part, c] for c in range(COLS)], axis=1)
            image = permuted(image, matrix)
            for c in range(COLS):
                out[part, c] = image[:, lane_block(c)]


def fields_kernel(probe, kappa, out, matrix):
    step = pl.program_id(0)

    @pl.when(step == 0)
    def _():
        matrix[...] = interleave()

    @pl.when(step < 2)
    def _():
        load_wrapped(out, (0,), permuted(probe[0], matrix[...]))

    @pl.when(step == 2)
    def _():
        load_wrapped(out, (0,), permuted(kappa[...], matrix[...]))


def frames_kernel(
    strip_index,
    partial,
    before,
    after,
    measured,
    fields,
    facts,
    out,
    known_out,
    wrapped,
    arrival,
    window,
    local,
    field_a,
    field_b,
    field_c,
    total,
    positions,
):
    pad = 8
    copy = pltpu.make_async_copy(fields.at[pl.ds(0, 3)], wrapped, arrival)
    copy.start()
    known = facts[...]
    for frame in range(FRAMES):
        for k in range(2):
            place = measured[frame, 0, k : k + 1]
            positions[frame, k] = jnp.max(place).astype(jnp.int32)
            known = jnp.where(lane_ids(1) == 2 * frame + k, place, known)
    known_out[...] = jnp.broadcast_to(known, known_out.shape)
    window[...] = partial[:, :, SH - BASE : SH - BASE + ROWS]
    window[:, :, :SENT] += before[...]
    window[:, :, ROWS - SENT :] += after[...]
    total[...] = jnp.zeros_like(total)
    for field in (field_a, field_b, field_c):
        field[:, :, :pad] = jnp.zeros((2, COLS, pad, LANES), F32)
        field[:, :, pad + ROWS :] = jnp.zeros((2, COLS, pad, LANES), F32)
    tile = 16

    def laplace(field, part, row, tile=tile):
        centre = field[part, :, pl.ds(row, tile)]
        around = field[part, :, pl.ds(row - 1, tile)] + field[part, :, pl.ds(row + 1, tile)]
        left = jnp.concatenate([pltpu.roll(centre[COLS - 1 :], 1, 2), centre[: COLS - 1]], axis=0)
        right = jnp.concatenate([centre[1:], pltpu.roll(centre[:1], LANES - 1, 2)], axis=0)
        return centre, around + left + right - 4.0 * centre

    def per_frame(frame, _):
        first_row = (strip_index[0] * STRIP - BASE - positions[frame, 0]) & (NX - 1)
        for k in range(3):
            for c, block in enumerate(
                interleaved_roll(wrapped, (k,), first_row, ROWS, positions[frame, 1])
            ):
                local[k, c] = block
        tiles = range(0, ROWS, tile)
        for row in tiles:
            rows, padded = pl.ds(row, tile), pl.ds(row + pad, tile)
            probe_re, probe_im = local[0, :, rows], local[1, :, rows]
            re, im = window[0, :, rows], window[1, :, rows]
            field_a[0, :, padded] = probe_re * re - probe_im * im
            field_a[1, :, padded] = probe_re * im + probe_im * re
        for row in tiles:
            rows, padded = pl.ds(row, tile), pl.ds(row + pad, tile)
            re, lap_re = laplace(field_a, 0, row + pad)
            im, lap_im = laplace(field_a, 1, row + pad)
            kappa = local[2, :, rows]
            field_b[0, :, padded] = re - kappa * lap_im
            field_b[1, :, padded] = im + kappa * lap_re
        for seen in range(0, SEEN_ROWS, 8):
            row = seen + BASE - SEEN_BASE
            rows, padded = pl.ds(row, 8), pl.ds(row + pad, 8)
            re, lap_re = laplace(field_b, 0, row + pad, 8)
            im, lap_im = laplace(field_b, 1, row + pad, 8)
            kappa = local[2, :, rows]
            wave_re = re - kappa * lap_im
            wave_im = im + kappa * lap_re
            twice = 2.0 * (wave_re * wave_re + wave_im * wave_im - measured[frame, :, pl.ds(seen, 8)])
            grad_re, grad_im = twice * wave_re, twice * wave_im
            field_a[0, :, padded] = grad_re
            field_a[1, :, padded] = grad_im
            field_c[0, :, padded] = kappa * grad_re
            field_c[1, :, padded] = kappa * grad_im
        for row in tiles:
            rows, padded = pl.ds(row, tile), pl.ds(row + pad, tile)
            _, lap_re = laplace(field_c, 0, row + pad)
            _, lap_im = laplace(field_c, 1, row + pad)
            kappa = local[2, :, rows]
            grad_re = field_a[0, :, padded] + lap_im
            grad_im = field_a[1, :, padded] - lap_re
            field_a[0, :, padded] = grad_re
            field_a[1, :, padded] = grad_im
            field_b[0, :, padded] = kappa * grad_re
            field_b[1, :, padded] = kappa * grad_im
        for row in range(0, STRIP, tile):
            rows, padded = pl.ds(row + BASE, tile), pl.ds(row + BASE + pad, tile)
            _, lap_re = laplace(field_b, 0, row + BASE + pad)
            _, lap_im = laplace(field_b, 1, row + BASE + pad)
            grad_re = field_a[0, :, padded] + lap_im
            grad_im = field_a[1, :, padded] - lap_re
            probe_re, probe_im = local[0, :, rows], local[1, :, rows]
            total[0, :, pl.ds(row, tile)] += probe_re * grad_re + probe_im * grad_im
            total[1, :, pl.ds(row, tile)] += probe_re * grad_im - probe_im * grad_re
        return 0

    copy.wait()
    lax.fori_loop(0, FRAMES, per_frame, 0)
    matrix = interleave(transposed=True)
    for part in range(2):
        image = jnp.concatenate([total[part, c] for c in range(COLS)], axis=1)
        image = permuted(image, matrix)
        for c in range(COLS):
            rows = pl.ds(part * COLS + c, STRIP, stride=BLOCKS)
            out[rows, :] = image[:, lane_block(c)]


def gather_weights(strip_index, positions, probe, out, wrapped):
    load_wrapped(wrapped, (), probe[0] * probe[0] + probe[1] * probe[1])
    chunk = 32

    keeps = lane_ids(chunk)

    def per_angle(angle, _):
        firsts, wholes, parts = [], [], []
        for frame in range(FRAMES):
            top, amount = positions[angle, 2 * frame], positions[angle, 2 * frame + 1]
            firsts.append((strip_index[0] * STRIP - SH - top) & (NX - 1))
            wholes.append(amount >> 7)
            parts.append(amount & (LANES - 1))
        for row in range(0, RIM_ROWS, chunk):
            total = [jnp.zeros((chunk, LANES), F32)] * COLS
            for first, whole, part in zip(firsts, wholes, parts):
                turned = [
                    pltpu.roll(
                        wrapped[(c - whole) & (COLS - 1), pl.ds(first + row, chunk)], part, 1
                    )
                    for c in range(COLS)
                ]
                keep = keeps >= part
                total = [
                    total[c] + jnp.where(keep, turned[c], turned[c - 1]) for c in range(COLS)
                ]
            for c in range(COLS):
                out[angle, c, row : row + chunk] = total[c]
        return 0

    lax.fori_loop(0, ANGLES, per_angle, 0)


def divisor_kernel(
    strip_index,
    positions,
    shears,
    probe,
    own,
    slices,
    out,
    rest,
    weights,
    wrapped,
    grads,
    rows,
):
    @pl.when(pl.program_id(0) == 0)
    def _():
        gather_weights(strip_index, positions, probe, weights, wrapped)
        fill_grads(grads, (own,))

    base = pl.program_id(0) * out.shape[0]

    def per_slice(k, _):
        starts = [SH - shears[a, base + k] for a in range(ANGLES)]
        for c in range(COLS):
            total = jnp.ones((STRIP, LANES), F32)
            for a in range(ANGLES):
                total += weights[a, c, pl.ds(starts[a], STRIP)]
            out[k, :, lane_block(c)] = 1.0 / total
        take_grads(starts[:SIDE], grads, rows, slices.at[k], out.at[k], rest.at[k])
        return 0

    lax.fori_loop(0, out.shape[0], per_slice, 0)


def split(values):
    high = values.astype(BF16)
    return high, (values - high.astype(F32)).astype(BF16)


def pack_kernel(*refs):
    last, first = refs[-2:]
    for k in range(2):

        @pl.when(pl.program_id(0) == k)
        def _():
            last[...] = refs[2 * k][...]
            first[...] = refs[2 * k + 1][...]


def pack(pieces, places, rims):
    edge = (SIDE, SH, BLOCKS, LANES)
    ends = [
        pl.BlockSpec(edge, lambda i: (0, STRIP // SH - 1, 0, 0)),
        pl.BlockSpec(edge, lambda i: (0, 0, 0, 0)),
    ]
    start, stride = places[0], places[1] - places[0]
    return pl.pallas_call(
        pack_kernel,
        grid=(2,),
        out_shape=[jax.ShapeDtypeStruct((ANGLES, SH, BLOCKS, LANES), F32)] * 2,
        in_specs=ends * 2 + [pl.BlockSpec(memory_space=pl.ANY)] * len(rims),
        out_specs=[pl.BlockSpec(edge, lambda i: (start + i * stride, 0, 0, 0))] * 2,
        input_output_aliases={4 + k: k for k in range(len(rims))},
        compiler_params=vmem(12),
        cost_estimate=cost(1),
        name="pack",
    )(pieces[0], pieces[0], pieces[1], pieces[1], *rims)


def fill_grads(grads, pieces):
    for k, piece in enumerate(pieces):
        grads[SIDE * k : SIDE * (k + 1), SH : SH + STRIP] = piece[...]
    count = SIDE * len(pieces)
    grads[:, :SH] = jnp.zeros((count, SH, BLOCKS, LANES), F32)
    grads[:, SH + STRIP :] = jnp.zeros((count, SH, BLOCKS, LANES), F32)


def take_grads(starts, grads, rows, slices, scale, out):
    chunk = 8
    for row in range(0, STRIP, chunk):
        total = grads[0, pl.ds(starts[0] + row, chunk)]
        for a in range(1, len(starts)):
            total += grads[a, pl.ds(starts[a] + row, chunk)]
        rows[row * BLOCKS : (row + chunk) * BLOCKS] = total.reshape(chunk * BLOCKS, LANES)
    for part in range(2):
        for c in range(COLS):
            total = rows[pl.ds(part * COLS + c, STRIP, stride=BLOCKS), :]
            cols = lane_block(c)
            out[part, :, cols] = slices[part, :, cols] - total * scale[:, cols]


def core_kernel(shears, two, one, three, slices, scale, out, grads, rows):
    @pl.when(pl.program_id(0) == 0)
    def _():
        fill_grads(grads, (two, one, three))

    count = out.shape[0]
    base = pl.program_id(0) * count
    for k in range(count):
        starts = [SH - shears[a, base + k] for a in range(SIDE, ANGLES)]
        take_grads(
            starts, grads, rows.at[k], slices.at[k], scale.at[k], out.at[k]
        )


def rim_kernel(shears, before, after, scale, core, out, high, low, shifts):
    side = pl.program_id(0)

    def take(rim):
        for a in range(ANGLES):
            for part in range(2):
                for c in range(COLS):
                    rows, cols = slice(a * SH, (a + 1) * SH), lane_block(part * COLS + c)
                    block = part * COLS + c
                    picked = pl.ds(a * SH * BLOCKS + block, SH, stride=BLOCKS)
                    high[rows, cols], low[rows, cols] = split(rim[picked, :])

    @pl.when((pl.program_id(1) == 0) & (side == 0))
    def _():
        take(before)

    @pl.when((pl.program_id(1) == 0) & (side == 1))
    def _():
        take(after)

    count = out.shape[0]
    width = ANGLES * SH
    column = lax.broadcasted_iota(jnp.int32, (SH, width), 1) & (SH - 1)
    apart = column - lax.broadcasted_iota(jnp.int32, (SH, width), 0)
    middle = jnp.where(side == 0, SH, -SH)
    for k in range(count):
        chosen = jnp.where(apart == middle - shears[k : k + 1], 1.0, 0.0)
        shifts[k * SH : (k + 1) * SH] = chosen.astype(BF16)
    product = jnp.dot(shifts[...], high[...], preferred_element_type=F32)
    product += jnp.dot(shifts[...], low[...], preferred_element_type=F32)
    for k in range(count):
        for part in range(2):
            total = product[k * SH : (k + 1) * SH, part * NY : (part + 1) * NY]
            out[k, part] = core[k, part] - total * scale[k]


def hop_pairs(hop, stage):
    pairs = []
    for y in range(SIDE):
        for x in range(SIDE):
            for block in range(FRAMES):
                along_x = (block % 2 == 0) == (stage == 0)
                to_y = y if along_x else (y + hop) % SIDE
                to_x = (x + hop) % SIDE if along_x else x
                pairs.append(((y * SIDE + x) * FRAMES + block, (to_y * SIDE + to_x) * FRAMES + block))
    return pairs


def gather_angles(grads, facts):
    axes = ("angle", "block")
    facts = lax.all_to_all(facts, "angle", 0, 0)[:, 0]
    row = jnp.stack([grads] + [lax.ppermute(grads, axes, hop_pairs(hop, 0)) for hop in HOPS])
    row, facts = lax.optimization_barrier((row, facts))
    pieces = [row] + [lax.ppermute(row, axes, hop_pairs(hop, 1)) for hop in HOPS]
    angle = lax.axis_index("angle")
    odd = lax.axis_index("block") % 2
    first, second = jnp.asarray((0,) + HOPS), jnp.asarray((0,) + HOPS)
    along_x = jnp.where(odd == 1, second[:, None], first[None])
    along_y = jnp.where(odd == 1, first[None], second[:, None])
    order = ((angle // SIDE - along_y) % SIDE) * SIDE + (angle - along_x) % SIDE
    return pieces, order.reshape(ANGLES), facts.astype(jnp.int32)


def per_device(object_field, shears, positions, measured, probe_field, kappa_field):
    strip_index = lax.axis_index("block").astype(jnp.int32)[None]
    moved = pl.pallas_call(
        measured_kernel,
        out_shape=jax.ShapeDtypeStruct((FRAMES, COLS, SEEN_ROWS, LANES), F32),
        in_specs=[SMEM, VMEM],
        out_specs=VMEM,
        scratch_shapes=[pltpu.VMEM((COLS, WRAP, LANES), F32)],
        compiler_params=vmem(60),
        cost_estimate=cost(3),
        name="measured_rows",
    )(positions[0, 0], measured[0, 0])
    observed = lax.all_to_all(moved, "block", 0, 0)
    step = 8
    partial = pl.pallas_call(
        project_kernel,
        grid=(Z // step,),
        out_shape=jax.ShapeDtypeStruct((2, COLS, RIM_ROWS, LANES), F32),
        in_specs=[SMEM, pl.BlockSpec((step, 2, STRIP, NY), lambda i: (i, 0, 0, 0))],
        out_specs=pl.BlockSpec((2, COLS, RIM_ROWS, LANES), lambda i: (0, 0, 0, 0)),
        compiler_params=vmem(60),
        cost_estimate=cost(7),
        name="project",
    )(shears[0], object_field)
    step = 4
    count = FRAMES
    up = [(i, (i + 1) % count) for i in range(count)]
    down = [(j, i) for i, j in up]
    before = lax.ppermute(partial[:, :, RIM_ROWS - SENT :], "block", up)
    after = lax.ppermute(partial[:, :, :SENT], "block", down)
    wrapped = pl.pallas_call(
        fields_kernel,
        grid=(3,),
        out_shape=jax.ShapeDtypeStruct((3 * SPARE, COLS, WRAP, LANES), F32),
        in_specs=[
            pl.BlockSpec((1, NX, NY), lambda i: (jnp.minimum(i, 1), 0, 0)),
            pl.BlockSpec((NX, NY), lambda i: (0, 0)),
        ],
        out_specs=pl.BlockSpec((1, COLS, WRAP, LANES), lambda i: (i, 0, 0, 0)),
        scratch_shapes=[pltpu.VMEM((NY, NY), BF16)],
        compiler_params=vmem(60),
        cost_estimate=cost(6),
        name="fields",
    )(probe_field, kappa_field[0])

    facts = jnp.pad(shears.astype(F32), ((0, 0), (2 * FRAMES, LANES - 2 * FRAMES - Z)))
    field = pltpu.VMEM((2, COLS, ROWS + 16, LANES), F32)
    grads, facts = pl.pallas_call(
        frames_kernel,
        out_shape=[
            jax.ShapeDtypeStruct((STRIP * BLOCKS, LANES), F32),
            jax.ShapeDtypeStruct((ANGLES * 8, LANES), F32),
        ],
        in_specs=[SMEM] + [VMEM] * 4 + [pl.BlockSpec(memory_space=pltpu.HBM), VMEM],
        out_specs=[VMEM, VMEM],
        scratch_shapes=[
            pltpu.VMEM((3, COLS, WRAP, LANES), F32),
            pltpu.SemaphoreType.DMA,
            pltpu.VMEM((2, COLS, ROWS, LANES), F32),
            pltpu.VMEM((3, COLS, ROWS, LANES), F32),
            field,
            field,
            field,
            pltpu.VMEM((2, COLS, STRIP, LANES), F32),
            pltpu.SMEM((FRAMES, 2), jnp.int32),
        ],
        compiler_params=vmem(15),
        cost_estimate=cost(9),
        name="frames",
    )(strip_index, partial, before, after, observed, wrapped, facts)
    pieces, order, facts = gather_angles(
        grads.reshape(STRIP, BLOCKS, LANES), facts.reshape(ANGLES, 8, LANES)
    )
    facts = jnp.take(facts, order, axis=0)
    all_positions = facts[:, : 2 * FRAMES]
    all_shears = facts[:, 2 * FRAMES : 2 * FRAMES + Z]
    rim_shears = all_shears.reshape(SIDE, SIDE, Z).transpose(2, 1, 0).reshape(Z, ANGLES)
    rim_shears = jnp.repeat(rim_shears, SH, axis=1)

    slices_spec = pl.BlockSpec((step, STRIP, NY), lambda i: (i, 0, 0))
    own, two, one, three = pieces
    object_spec = pl.BlockSpec((step, 2, STRIP, NY), lambda i: (i, 0, 0, 0))
    scale, rest = pl.pallas_call(
        divisor_kernel,
        grid=(Z // step,),
        out_shape=[
            jax.ShapeDtypeStruct((Z, STRIP, NY), F32),
            jax.ShapeDtypeStruct(object_field.shape, F32),
        ],
        in_specs=[SMEM, SMEM, SMEM, VMEM, VMEM, object_spec],
        out_specs=[slices_spec, object_spec],
        scratch_shapes=[
            pltpu.VMEM((ANGLES, COLS, RIM_ROWS, LANES), F32),
            pltpu.VMEM((COLS, WRAP, LANES), F32),
            pltpu.VMEM((SIDE, RIM_ROWS, BLOCKS, LANES), F32),
            pltpu.VMEM((STRIP * BLOCKS, LANES), F32),
        ],
        compiler_params=vmem(60),
        cost_estimate=cost(2),
        name="divisor",
    )(strip_index, all_positions, all_shears, probe_field, own, object_field)

    scale, rim_shears, own, three = lax.optimization_barrier((scale, rim_shears, own, three))
    rims = pack((own, three), (0, 3), ())
    rims = pack((two, one), (1, 2), rims)
    pieces = (two, one, three)
    rims = [
        lax.ppermute(rim, "block", pairs).reshape(ANGLES * SH * BLOCKS, LANES)
        for rim, pairs in zip(rims, (up, down))
    ]

    step = 8
    slices_spec = pl.BlockSpec((step, STRIP, NY), lambda i: (i, 0, 0))
    object_spec = pl.BlockSpec((step, 2, STRIP, NY), lambda i: (i, 0, 0, 0))
    core = pl.pallas_call(
        core_kernel,
        grid=(Z // step,),
        out_shape=jax.ShapeDtypeStruct(object_field.shape, F32),
        in_specs=[SMEM] + [VMEM] * 3 + [object_spec, slices_spec],
        out_specs=object_spec,
        scratch_shapes=[
            pltpu.VMEM((ANGLES - SIDE, RIM_ROWS, BLOCKS, LANES), F32),
            pltpu.VMEM((step, STRIP * BLOCKS, LANES), F32),
        ],
        compiler_params=vmem(50),
        cost_estimate=cost(17),
        name="core",
    )(all_shears, *pieces, rest, scale)
    many = 32
    edge_spec = pl.BlockSpec((many, 2, SH, NY), lambda j, i: (i, 0, j * (STRIP // SH - 1), 0))
    return pl.pallas_call(
        rim_kernel,
        grid=(2, Z // many),
        out_shape=jax.ShapeDtypeStruct(object_field.shape, F32),
        in_specs=[pl.BlockSpec((many, ANGLES * SH), lambda j, i: (i, 0)), VMEM, VMEM]
        + [pl.BlockSpec((many, SH, NY), lambda j, i: (i, j * (STRIP // SH - 1), 0)), edge_spec],
        out_specs=edge_spec,
        scratch_shapes=[
            pltpu.VMEM((ANGLES * SH, 2 * NY), BF16),
            pltpu.VMEM((ANGLES * SH, 2 * NY), BF16),
            pltpu.VMEM((many * SH, ANGLES * SH), BF16),
        ],
        input_output_aliases={4: 0},
        compiler_params=vmem(50),
        cost_estimate=cost(9),
        name="rim",
    )(rim_shears, *rims, scale, core)


def solution(mesh):
    placed = (
        P(None, None, "block", None),
        P("angle", None),
        P("angle", "block", None),
        P("angle", "block", None, None),
        P(),
        P("angle", None, None),
    )
    return jax.shard_map(
        per_device,
        mesh=mesh,
        in_specs=placed,
        out_specs=P(None, None, "block", None),
        check_vma=False,
    )
```

```python
import jax
import jax.numpy as jnp
from jax import lax
from jax.experimental import pallas as pl
from jax.experimental.pallas import tpu as pltpu
from jax.sharding import PartitionSpec as P

NX = 512
NY = 512
Z = 32
SH = 16
ANGLES = 16
FRAMES = 8
STRIP = 64
LANES = 128
COLS = NY // LANES
BASE = 8
ROWS = STRIP + 2 * BASE
SEEN_BASE = 4
SEEN_ROWS = STRIP + 2 * SEEN_BASE
RIM_ROWS = STRIP + 2 * SH
SENT = BASE + SH
WRAP = NX + RIM_ROWS
F32 = jnp.float32
BF16 = jnp.bfloat16
HOPS = (2, 1, 3)
SIDE = 4
SPARE = 16
BLOCKS = 2 * COLS
COST_SCALE = 3_000_000

SMEM = pl.BlockSpec(memory_space=pltpu.SMEM)
VMEM = pl.BlockSpec(memory_space=pltpu.VMEM)


def cost(microseconds):
    return pl.CostEstimate(
        flops=0, transcendentals=0, bytes_accessed=microseconds * COST_SCALE
    )


def vmem(mebibytes):
    return pltpu.CompilerParams(vmem_limit_bytes=mebibytes * 2**20)


def lane_block(c):
    return slice(c * LANES, (c + 1) * LANES)


def lane_ids(rows):
    return lax.broadcasted_iota(jnp.int32, (rows, LANES), 1)


def load_wrapped(scratch, index, image):
    for c in range(COLS):
        scratch[index + (c, pl.ds(0, NX))] = image[:, lane_block(c)]
        scratch[index + (c, pl.ds(NX, WRAP - NX))] = image[: WRAP - NX, lane_block(c)]


def interleave(transposed=False):
    old = lax.broadcasted_iota(jnp.int32, (NY, NY), 1 if transposed else 0)
    new = lax.broadcasted_iota(jnp.int32, (NY, NY), 0 if transposed else 1)
    return jnp.where(old == (new % LANES) * COLS + new // LANES, 1.0, 0.0).astype(BF16)


def permuted(image, matrix):
    result = None
    for term in range(3):
        high = image.astype(BF16)
        product = jnp.dot(high, matrix, preferred_element_type=F32)
        result = product if result is None else result + product
        if term < 2:
            image = image - high.astype(F32)
    return result


def interleaved_roll(scratch, index, first_row, rows, amount):
    whole, part = amount >> 2, amount & (COLS - 1)
    return [
        pltpu.roll(
            scratch[index + ((c - part) & (COLS - 1), pl.ds(first_row, rows))],
            (whole + jnp.where(c < part, 1, 0)) & (LANES - 1),
            1,
        )
        for c in range(COLS)
    ]


def measured_kernel(position, measured, out, wrapped):
    load_wrapped(
        wrapped, (), jnp.dot(measured[...], interleave(), preferred_element_type=F32)
    )
    for strip in range(FRAMES):
        first_row = (strip * STRIP - SEEN_BASE - position[0]) & (NX - 1)
        for c, block in enumerate(interleaved_roll(wrapped, (), first_row, SEEN_ROWS, position[1])):
            out[strip, c] = block
        for k in range(2):
            out[strip, 0, k : k + 1] = jnp.full((1, LANES), position[k].astype(F32), F32)


def project_kernel(shears, slices, out):
    step = pl.program_id(0)

    @pl.when(step == 0)
    def _():
        out[...] = jnp.zeros_like(out)

    count = slices.shape[0]
    for k in range(count):
        rows = pl.ds(SH - shears[step * count + k], STRIP)
        for part in range(2):
            for c in range(COLS):
                out[part, c, rows] += slices[k, part, :, lane_block(c)]

    @pl.when(step == pl.num_programs(0) - 1)
    def _():
        matrix = interleave()
        for part in range(2):
            image = jnp.concatenate([out[part, c] for c in range(COLS)], axis=1)
            image = permuted(image, matrix)
            for c in range(COLS):
                out[part, c] = image[:, lane_block(c)]


def fields_kernel(probe, kappa, out, matrix):
    step = pl.program_id(0)

    @pl.when(step == 0)
    def _():
        matrix[...] = interleave()

    @pl.when(step < 2)
    def _():
        load_wrapped(out, (0,), permuted(probe[0], matrix[...]))

    @pl.when(step == 2)
    def _():
        load_wrapped(out, (0,), permuted(kappa[...], matrix[...]))


def frames_kernel(
    strip_index,
    partial,
    before,
    after,
    measured,
    fields,
    facts,
    out,
    known_out,
    wrapped,
    arrival,
    window,
    local,
    field_a,
    field_b,
    field_c,
    total,
    positions,
):
    pad = 8
    copy = pltpu.make_async_copy(fields.at[pl.ds(0, 3)], wrapped, arrival)
    copy.start()
    known = facts[...]
    for frame in range(FRAMES):
        for k in range(2):
            place = measured[frame, 0, k : k + 1]
            positions[frame, k] = jnp.max(place).astype(jnp.int32)
            known = jnp.where(lane_ids(1) == 2 * frame + k, place, known)
    known_out[...] = jnp.broadcast_to(known, known_out.shape)
    window[...] = partial[:, :, SH - BASE : SH - BASE + ROWS]
    window[:, :, :SENT] += before[...]
    window[:, :, ROWS - SENT :] += after[...]
    total[...] = jnp.zeros_like(total)
    for field in (field_a, field_b, field_c):
        field[:, :, :pad] = jnp.zeros((2, COLS, pad, LANES), F32)
        field[:, :, pad + ROWS :] = jnp.zeros((2, COLS, pad, LANES), F32)
    tile = 16

    def laplace(field, part, row, tile=tile):
        centre = field[part, :, pl.ds(row, tile)]
        around = field[part, :, pl.ds(row - 1, tile)] + field[part, :, pl.ds(row + 1, tile)]
        left = jnp.concatenate([pltpu.roll(centre[COLS - 1 :], 1, 2), centre[: COLS - 1]], axis=0)
        right = jnp.concatenate([centre[1:], pltpu.roll(centre[:1], LANES - 1, 2)], axis=0)
        return centre, around + left + right - 4.0 * centre

    def per_frame(frame, _):
        first_row = (strip_index[0] * STRIP - BASE - positions[frame, 0]) & (NX - 1)
        for k in range(3):
            for c, block in enumerate(
                interleaved_roll(wrapped, (k,), first_row, ROWS, positions[frame, 1])
            ):
                local[k, c] = block
        tiles = range(0, ROWS, tile)
        for row in tiles:
            rows, padded = pl.ds(row, tile), pl.ds(row + pad, tile)
            probe_re, probe_im = local[0, :, rows], local[1, :, rows]
            re, im = window[0, :, rows], window[1, :, rows]
            field_a[0, :, padded] = probe_re * re - probe_im * im
            field_a[1, :, padded] = probe_re * im + probe_im * re
        for row in tiles:
            rows, padded = pl.ds(row, tile), pl.ds(row + pad, tile)
            re, lap_re = laplace(field_a, 0, row + pad)
            im, lap_im = laplace(field_a, 1, row + pad)
            kappa = local[2, :, rows]
            field_b[0, :, padded] = re - kappa * lap_im
            field_b[1, :, padded] = im + kappa * lap_re
        for seen in range(0, SEEN_ROWS, 8):
            row = seen + BASE - SEEN_BASE
            rows, padded = pl.ds(row, 8), pl.ds(row + pad, 8)
            re, lap_re = laplace(field_b, 0, row + pad, 8)
            im, lap_im = laplace(field_b, 1, row + pad, 8)
            kappa = local[2, :, rows]
            wave_re = re - kappa * lap_im
            wave_im = im + kappa * lap_re
            twice = 2.0 * (wave_re * wave_re + wave_im * wave_im - measured[frame, :, pl.ds(seen, 8)])
            grad_re, grad_im = twice * wave_re, twice * wave_im
            field_a[0, :, padded] = grad_re
            field_a[1, :, padded] = grad_im
            field_c[0, :, padded] = kappa * grad_re
            field_c[1, :, padded] = kappa * grad_im
        for row in tiles:
            rows, padded = pl.ds(row, tile), pl.ds(row + pad, tile)
            _, lap_re = laplace(field_c, 0, row + pad)
            _, lap_im = laplace(field_c, 1, row + pad)
            kappa = local[2, :, rows]
            grad_re = field_a[0, :, padded] + lap_im
            grad_im = field_a[1, :, padded] - lap_re
            field_a[0, :, padded] = grad_re
            field_a[1, :, padded] = grad_im
            field_b[0, :, padded] = kappa * grad_re
            field_b[1, :, padded] = kappa * grad_im
        for row in range(0, STRIP, tile):
            rows, padded = pl.ds(row + BASE, tile), pl.ds(row + BASE + pad, tile)
            _, lap_re = laplace(field_b, 0, row + BASE + pad)
            _, lap_im = laplace(field_b, 1, row + BASE + pad)
            grad_re = field_a[0, :, padded] + lap_im
            grad_im = field_a[1, :, padded] - lap_re
            probe_re, probe_im = local[0, :, rows], local[1, :, rows]
            total[0, :, pl.ds(row, tile)] += probe_re * grad_re + probe_im * grad_im
            total[1, :, pl.ds(row, tile)] += probe_re * grad_im - probe_im * grad_re
        return 0

    copy.wait()
    lax.fori_loop(0, FRAMES, per_frame, 0)
    matrix = interleave(transposed=True)
    for part in range(2):
        image = jnp.concatenate([total[part, c] for c in range(COLS)], axis=1)
        image = permuted(image, matrix)
        for c in range(COLS):
            rows = pl.ds(part * COLS + c, STRIP, stride=BLOCKS)
            out[rows, :] = image[:, lane_block(c)]


def gather_weights(strip_index, positions, probe, out, wrapped):
    load_wrapped(wrapped, (), probe[0] * probe[0] + probe[1] * probe[1])
    chunk = 32

    keeps = lane_ids(chunk)

    def per_angle(angle, _):
        firsts, wholes, parts = [], [], []
        for frame in range(FRAMES):
            top, amount = positions[angle, 2 * frame], positions[angle, 2 * frame + 1]
            firsts.append((strip_index[0] * STRIP - SH - top) & (NX - 1))
            wholes.append(amount >> 7)
            parts.append(amount & (LANES - 1))
        for row in range(0, RIM_ROWS, chunk):
            total = [jnp.zeros((chunk, LANES), F32)] * COLS
            for first, whole, part in zip(firsts, wholes, parts):
                turned = [
                    pltpu.roll(
                        wrapped[(c - whole) & (COLS - 1), pl.ds(first + row, chunk)], part, 1
                    )
                    for c in range(COLS)
                ]
                keep = keeps >= part
                total = [
                    total[c] + jnp.where(keep, turned[c], turned[c - 1]) for c in range(COLS)
                ]
            for c in range(COLS):
                out[angle, c, row : row + chunk] = total[c]
        return 0

    lax.fori_loop(0, ANGLES, per_angle, 0)


def divisor_kernel(
    strip_index,
    positions,
    shears,
    probe,
    own,
    slices,
    out,
    rest,
    weights,
    wrapped,
    grads,
    rows,
):
    @pl.when(pl.program_id(0) == 0)
    def _():
        gather_weights(strip_index, positions, probe, weights, wrapped)
        fill_grads(grads, (own,))

    base = pl.program_id(0) * out.shape[0]

    def per_slice(k, _):
        starts = [SH - shears[a, base + k] for a in range(ANGLES)]
        for c in range(COLS):
            total = jnp.ones((STRIP, LANES), F32)
            for a in range(ANGLES):
                total += weights[a, c, pl.ds(starts[a], STRIP)]
            out[k, :, lane_block(c)] = 1.0 / total
        take_grads(starts[:SIDE], grads, rows, slices.at[k], out.at[k], rest.at[k])
        return 0

    lax.fori_loop(0, out.shape[0], per_slice, 0)


def split(values):
    high = values.astype(BF16)
    return high, (values - high.astype(F32)).astype(BF16)


def pack_kernel(*refs):
    last, first = refs[-2:]
    for k in range(2):

        @pl.when(pl.program_id(0) == k)
        def _():
            last[...] = refs[2 * k][...]
            first[...] = refs[2 * k + 1][...]


def pack(pieces, places, rims):
    edge = (SIDE, SH, BLOCKS, LANES)
    ends = [
        pl.BlockSpec(edge, lambda i: (0, STRIP // SH - 1, 0, 0)),
        pl.BlockSpec(edge, lambda i: (0, 0, 0, 0)),
    ]
    start, stride = places[0], places[1] - places[0]
    return pl.pallas_call(
        pack_kernel,
        grid=(2,),
        out_shape=[jax.ShapeDtypeStruct((ANGLES, SH, BLOCKS, LANES), F32)] * 2,
        in_specs=ends * 2 + [pl.BlockSpec(memory_space=pl.ANY)] * len(rims),
        out_specs=[pl.BlockSpec(edge, lambda i: (start + i * stride, 0, 0, 0))] * 2,
        input_output_aliases={4 + k: k for k in range(len(rims))},
        compiler_params=vmem(12),
        cost_estimate=cost(1),
        name="pack",
    )(pieces[0], pieces[0], pieces[1], pieces[1], *rims)


def fill_grads(grads, pieces):
    for k, piece in enumerate(pieces):
        grads[SIDE * k : SIDE * (k + 1), SH : SH + STRIP] = piece[...]
    count = SIDE * len(pieces)
    grads[:, :SH] = jnp.zeros((count, SH, BLOCKS, LANES), F32)
    grads[:, SH + STRIP :] = jnp.zeros((count, SH, BLOCKS, LANES), F32)


def take_grads(starts, grads, rows, slices, scale, out):
    chunk = 8
    for row in range(0, STRIP, chunk):
        total = grads[0, pl.ds(starts[0] + row, chunk)]
        for a in range(1, len(starts)):
            total += grads[a, pl.ds(starts[a] + row, chunk)]
        rows[row * BLOCKS : (row + chunk) * BLOCKS] = total.reshape(chunk * BLOCKS, LANES)
    for part in range(2):
        for c in range(COLS):
            total = rows[pl.ds(part * COLS + c, STRIP, stride=BLOCKS), :]
            cols = lane_block(c)
            out[part, :, cols] = slices[part, :, cols] - total * scale[:, cols]


def core_kernel(shears, two, one, three, slices, scale, out, grads, rows):
    @pl.when(pl.program_id(0) == 0)
    def _():
        fill_grads(grads, (two, one, three))

    count = out.shape[0]
    base = pl.program_id(0) * count
    for k in range(count):
        starts = [SH - shears[a, base + k] for a in range(SIDE, ANGLES)]
        take_grads(
            starts, grads, rows.at[k], slices.at[k], scale.at[k], out.at[k]
        )


def rim_kernel(shears, before, after, scale, core, out, high, low, shifts):
    side = pl.program_id(0)

    def take(rim):
        for a in range(ANGLES):
            for part in range(2):
                for c in range(COLS):
                    rows, cols = slice(a * SH, (a + 1) * SH), lane_block(part * COLS + c)
                    block = part * COLS + c
                    picked = pl.ds(a * SH * BLOCKS + block, SH, stride=BLOCKS)
                    high[rows, cols], low[rows, cols] = split(rim[picked, :])

    @pl.when((pl.program_id(1) == 0) & (side == 0))
    def _():
        take(before)

    @pl.when((pl.program_id(1) == 0) & (side == 1))
    def _():
        take(after)

    count = out.shape[0]
    width = ANGLES * SH
    column = lax.broadcasted_iota(jnp.int32, (SH, width), 1) & (SH - 1)
    apart = column - lax.broadcasted_iota(jnp.int32, (SH, width), 0)
    middle = jnp.where(side == 0, SH, -SH)
    for k in range(count):
        chosen = jnp.where(apart == middle - shears[k : k + 1], 1.0, 0.0)
        shifts[k * SH : (k + 1) * SH] = chosen.astype(BF16)
    product = jnp.dot(shifts[...], high[...], preferred_element_type=F32)
    product += jnp.dot(shifts[...], low[...], preferred_element_type=F32)
    for k in range(count):
        for part in range(2):
            total = product[k * SH : (k + 1) * SH, part * NY : (part + 1) * NY]
            out[k, part] = core[k, part] - total * scale[k]


def hop_pairs(hop, stage):
    pairs = []
    for y in range(SIDE):
        for x in range(SIDE):
            for block in range(FRAMES):
                along_x = (block % 2 == 0) == (stage == 0)
                to_y = y if along_x else (y + hop) % SIDE
                to_x = (x + hop) % SIDE if along_x else x
                pairs.append(((y * SIDE + x) * FRAMES + block, (to_y * SIDE + to_x) * FRAMES + block))
    return pairs


def gather_angles(grads, facts):
    axes = ("angle", "block")
    facts = lax.all_to_all(facts, "angle", 0, 0)[:, 0]
    row = jnp.stack([grads] + [lax.ppermute(grads, axes, hop_pairs(hop, 0)) for hop in HOPS])
    row, facts = lax.optimization_barrier((row, facts))
    pieces = [row] + [lax.ppermute(row, axes, hop_pairs(hop, 1)) for hop in HOPS]
    angle = lax.axis_index("angle")
    odd = lax.axis_index("block") % 2
    first, second = jnp.asarray((0,) + HOPS), jnp.asarray((0,) + HOPS)
    along_x = jnp.where(odd == 1, second[:, None], first[None])
    along_y = jnp.where(odd == 1, first[None], second[:, None])
    order = ((angle // SIDE - along_y) % SIDE) * SIDE + (angle - along_x) % SIDE
    return pieces, order.reshape(ANGLES), facts.astype(jnp.int32)


def per_device(object_field, shears, positions, measured, probe_field, kappa_field):
    strip_index = lax.axis_index("block").astype(jnp.int32)[None]
    moved = pl.pallas_call(
        measured_kernel,
        out_shape=jax.ShapeDtypeStruct((FRAMES, COLS, SEEN_ROWS, LANES), F32),
        in_specs=[SMEM, VMEM],
        out_specs=VMEM,
        scratch_shapes=[pltpu.VMEM((COLS, WRAP, LANES), F32)],
        compiler_params=vmem(60),
        cost_estimate=cost(3),
        name="measured_rows",
    )(positions[0, 0], measured[0, 0])
    observed = lax.all_to_all(moved, "block", 0, 0)
    step = 8
    partial = pl.pallas_call(
        project_kernel,
        grid=(Z // step,),
        out_shape=jax.ShapeDtypeStruct((2, COLS, RIM_ROWS, LANES), F32),
        in_specs=[SMEM, pl.BlockSpec((step, 2, STRIP, NY), lambda i: (i, 0, 0, 0))],
        out_specs=pl.BlockSpec((2, COLS, RIM_ROWS, LANES), lambda i: (0, 0, 0, 0)),
        compiler_params=vmem(60),
        cost_estimate=cost(7),
        name="project",
    )(shears[0], object_field)
    step = 8
    count = FRAMES
    up = [(i, (i + 1) % count) for i in range(count)]
    down = [(j, i) for i, j in up]
    before = lax.ppermute(partial[:, :, RIM_ROWS - SENT :], "block", up)
    after = lax.ppermute(partial[:, :, :SENT], "block", down)
    wrapped = pl.pallas_call(
        fields_kernel,
        grid=(3,),
        out_shape=jax.ShapeDtypeStruct((3 * SPARE, COLS, WRAP, LANES), F32),
        in_specs=[
            pl.BlockSpec((1, NX, NY), lambda i: (jnp.minimum(i, 1), 0, 0)),
            pl.BlockSpec((NX, NY), lambda i: (0, 0)),
        ],
        out_specs=pl.BlockSpec((1, COLS, WRAP, LANES), lambda i: (i, 0, 0, 0)),
        scratch_shapes=[pltpu.VMEM((NY, NY), BF16)],
        compiler_params=vmem(60),
        cost_estimate=cost(6),
        name="fields",
    )(probe_field, kappa_field[0])

    facts = jnp.pad(shears.astype(F32), ((0, 0), (2 * FRAMES, LANES - 2 * FRAMES - Z)))
    field = pltpu.VMEM((2, COLS, ROWS + 16, LANES), F32)
    grads, facts = pl.pallas_call(
        frames_kernel,
        out_shape=[
            jax.ShapeDtypeStruct((STRIP * BLOCKS, LANES), F32),
            jax.ShapeDtypeStruct((ANGLES * 8, LANES), F32),
        ],
        in_specs=[SMEM] + [VMEM] * 4 + [pl.BlockSpec(memory_space=pltpu.HBM), VMEM],
        out_specs=[VMEM, VMEM],
        scratch_shapes=[
            pltpu.VMEM((3, COLS, WRAP, LANES), F32),
            pltpu.SemaphoreType.DMA,
            pltpu.VMEM((2, COLS, ROWS, LANES), F32),
            pltpu.VMEM((3, COLS, ROWS, LANES), F32),
            field,
            field,
            field,
            pltpu.VMEM((2, COLS, STRIP, LANES), F32),
            pltpu.SMEM((FRAMES, 2), jnp.int32),
        ],
        compiler_params=vmem(15),
        cost_estimate=cost(9),
        name="frames",
    )(strip_index, partial, before, after, observed, wrapped, facts)
    pieces, order, facts = gather_angles(
        grads.reshape(STRIP, BLOCKS, LANES), facts.reshape(ANGLES, 8, LANES)
    )
    facts = jnp.take(facts, order, axis=0)
    all_positions = facts[:, : 2 * FRAMES]
    all_shears = facts[:, 2 * FRAMES : 2 * FRAMES + Z]
    rim_shears = all_shears.reshape(SIDE, SIDE, Z).transpose(2, 1, 0).reshape(Z, ANGLES)
    rim_shears = jnp.repeat(rim_shears, SH, axis=1)

    slices_spec = pl.BlockSpec((step, STRIP, NY), lambda i: (i, 0, 0))
    own, two, one, three = pieces
    object_spec = pl.BlockSpec((step, 2, STRIP, NY), lambda i: (i, 0, 0, 0))
    scale, rest = pl.pallas_call(
        divisor_kernel,
        grid=(Z // step,),
        out_shape=[
            jax.ShapeDtypeStruct((Z, STRIP, NY), F32),
            jax.ShapeDtypeStruct(object_field.shape, F32),
        ],
        in_specs=[SMEM, SMEM, SMEM, VMEM, VMEM, object_spec],
        out_specs=[slices_spec, object_spec],
        scratch_shapes=[
            pltpu.VMEM((ANGLES, COLS, RIM_ROWS, LANES), F32),
            pltpu.VMEM((COLS, WRAP, LANES), F32),
            pltpu.VMEM((SIDE, RIM_ROWS, BLOCKS, LANES), F32),
            pltpu.VMEM((STRIP * BLOCKS, LANES), F32),
        ],
        compiler_params=vmem(60),
        cost_estimate=cost(2),
        name="divisor",
    )(strip_index, all_positions, all_shears, probe_field, own, object_field)

    scale, rim_shears, own, three = lax.optimization_barrier((scale, rim_shears, own, three))
    rims = pack((own, three), (0, 3), ())
    rims = pack((two, one), (1, 2), rims)
    pieces = (two, one, three)
    rims = [
        lax.ppermute(rim, "block", pairs).reshape(ANGLES * SH * BLOCKS, LANES)
        for rim, pairs in zip(rims, (up, down))
    ]

    step = 8
    slices_spec = pl.BlockSpec((step, STRIP, NY), lambda i: (i, 0, 0))
    object_spec = pl.BlockSpec((step, 2, STRIP, NY), lambda i: (i, 0, 0, 0))
    core = pl.pallas_call(
        core_kernel,
        grid=(Z // step,),
        out_shape=jax.ShapeDtypeStruct(object_field.shape, F32),
        in_specs=[SMEM] + [VMEM] * 3 + [object_spec, slices_spec],
        out_specs=object_spec,
        scratch_shapes=[
            pltpu.VMEM((ANGLES - SIDE, RIM_ROWS, BLOCKS, LANES), F32),
            pltpu.VMEM((step, STRIP * BLOCKS, LANES), F32),
        ],
        compiler_params=vmem(50),
        cost_estimate=cost(17),
        name="core",
    )(all_shears, *pieces, rest, scale)
    many = 32
    edge_spec = pl.BlockSpec((many, 2, SH, NY), lambda j, i: (i, 0, j * (STRIP // SH - 1), 0))
    return pl.pallas_call(
        rim_kernel,
        grid=(2, Z // many),
        out_shape=jax.ShapeDtypeStruct(object_field.shape, F32),
        in_specs=[pl.BlockSpec((many, ANGLES * SH), lambda j, i: (i, 0)), VMEM, VMEM]
        + [pl.BlockSpec((many, SH, NY), lambda j, i: (i, j * (STRIP // SH - 1), 0)), edge_spec],
        out_specs=edge_spec,
        scratch_shapes=[
            pltpu.VMEM((ANGLES * SH, 2 * NY), BF16),
            pltpu.VMEM((ANGLES * SH, 2 * NY), BF16),
            pltpu.VMEM((many * SH, ANGLES * SH), BF16),
        ],
        input_output_aliases={4: 0},
        compiler_params=vmem(50),
        cost_estimate=cost(9),
        name="rim",
    )(rim_shears, *rims, scale, core)


def solution(mesh):
    placed = (
        P(None, None, "block", None),
        P("angle", None),
        P("angle", "block", None),
        P("angle", "block", None, None),
        P(),
        P("angle", None, None),
    )
    return jax.shard_map(
        per_device,
        mesh=mesh,
        in_specs=placed,
        out_specs=P(None, None, "block", None),
        check_vma=False,
    )
```
